32 devices in a mesh: gx: 4 (over z), gy: 2 (over core), gz: 4 (over y, x).
Axes of the slice: x: 2, y: 2, z: 4, core: 2. Of those that a mesh axis runs over, the one named last changes fastest.
Arguments:
- density: float32 [64, 64, 256], P('gz', 'gx', 'gy'), may hold values from -8 to 8
Outputs:
- potential: float32 [64, 64, 256], P('gz', 'gx', 'gy')
- forces: float32 [3, 64, 64, 256], P(None, 'gz', 'gx', 'gy')
The draws below stay inside these ranges and needn't reach their ends.
All inputs are finite; a program needn't handle non-finite values.
Results may differ from the reference program's by a relative error of at most 0.0003.
Values sent between devices are 32-bit elements; how exact they have to be, the bound alone decides.
A program may use at most 64 MiB of HBM per device.

```python
import jax
import jax.numpy as jnp

RADIUS = 15
SCREEN = 32
NX = 64
NY = 64
NZ = 256
MX = 32
MY = 32
MZ = 128


def draw_density(key, part):
    key_noise, key_scale = jax.random.split(key, 2)
    rough_part = jax.random.normal(key_noise, (NX, NY, NZ), jnp.float32)
    factor = jnp.exp(jax.random.uniform(key_scale, (NX, NY, NZ), jnp.float32, -0.7, 0.7))
    values = rough_part * factor
    return jnp.clip(values, -8.0, 8.0)


def setup_inputs(seed: int = 0) -> dict:
    splits = jax.random.split(jax.random.key(seed), 2)
    density = draw_density(jax.random.fold_in(splits[1], 71), 0)
    return {"density": density}


WEIGHTS = (1.0, 0.7, 0.5)
FRACTIONS = (0.5, 0.25, 0.125)
AMPLITUDE = 2.0
SMOOTHING = 1.0

def profile(offset, spread):
    offsets = jnp.arange(-RADIUS, RADIUS + 1).astype(jnp.float32)
    norm_sum = jnp.sqrt(jnp.sum(jnp.exp(-offsets * offsets / (spread * spread))))
    inside = jnp.abs(offset) <= RADIUS
    return jnp.where(inside, jnp.exp(-offset * offset / (2.0 * spread * spread)), 0.0) / norm_sum

def periodic_vector(length, spread):
    indices = jnp.arange(length)
    signed = jnp.where(indices <= length // 2, indices, indices - length).astype(jnp.float32)
    return profile(signed, spread)

def short_range(density):
    spectrum = jnp.fft.rfftn(density)
    response = jnp.zeros((NX, NY, NZ // 2 + 1), jnp.float32)
    for fraction, weight in zip(FRACTIONS, WEIGHTS):
        spread = RADIUS * fraction
        along_x = jnp.fft.fft(periodic_vector(NX, spread)).real
        along_y = jnp.fft.fft(periodic_vector(NY, spread)).real
        along_z = jnp.fft.rfft(periodic_vector(NZ, spread)).real
        response = response + weight * along_x[:, None, None] * along_y[None, :, None] * along_z[None, None, :]
    return jnp.fft.irfftn(spectrum * response, s=(NX, NY, NZ))

def symbol(length):
    indices = jnp.arange(length)
    angles = jnp.pi * indices.astype(jnp.float32) / length
    return (4.0 * jnp.sin(angles) ** 2, indices == length // 2, indices == 0)

def prolong(values, which_axis):
    from_below = jnp.roll(values, 1, which_axis)
    from_above = jnp.roll(values, -1, which_axis)
    even_cells = 0.75 * values + 0.25 * from_below
    odd_cells = 0.75 * values + 0.25 * from_above
    joined = jnp.stack([even_cells, odd_cells], which_axis + 1)
    new_shape = list(values.shape)
    new_shape[which_axis] = 2 * new_shape[which_axis]
    return joined.reshape(new_shape)

def long_range(density):
    coarse = density.reshape(MX, 2, MY, 2, MZ, 2).mean(axis=(1, 3, 5))
    wave_x, edge_x, zero_x = symbol(MX)
    wave_y, edge_y, zero_y = symbol(MY)
    wave_z, edge_z, zero_z = symbol(MZ)
    kappa_sq = wave_x[:, None, None] + wave_y[None, :, None] + wave_z[None, None, :]
    dropped = edge_x[:, None, None] | edge_y[None, :, None] | edge_z[None, None, :]
    dropped = dropped | zero_x[:, None, None] & zero_y[None, :, None] & zero_z[None, None, :]
    green_fn = jnp.where(dropped, 0.0, AMPLITUDE * jnp.exp(-SMOOTHING * SMOOTHING * kappa_sq) / (kappa_sq + 1.0 / (SCREEN * SCREEN)))
    coarse_field = jnp.real(jnp.fft.ifftn(green_fn * jnp.fft.fftn(coarse)))
    for which_axis in range(3):
        coarse_field = prolong(coarse_field, which_axis)
    return coarse_field

def reference(density):
    potential = short_range(density) + long_range(density)
    forces = jnp.stack([-0.5 * (jnp.roll(potential, -1, which_axis) - jnp.roll(potential, 1, which_axis)) for which_axis in range(3)])
    return (potential, forces)
```

```python
import functools

import jax
import jax.numpy as jnp
import numpy as np
from jax import lax
from jax.experimental import pallas as pl
from jax.experimental.pallas import tpu as pltpu
from jax.sharding import PartitionSpec as P

RADIUS = 15
MARGIN = 16
SCREEN = 32


PRECISE = lax.Precision.HIGHEST
WEIGHTS = (1.0, 0.7, 0.5)
FRACTIONS = (0.5, 0.25, 0.125)
AMPLITUDE = 2.0
SMOOTHING = 1.0
TWO_PI = 6.283185307179586


def extended_2(cells, sides, width):
    for axis, dim in sides:
        count = lax.axis_size(axis)
        head = lax.slice_in_dim(cells, 0, width, axis=dim)
        tail = lax.slice_in_dim(cells, cells.shape[dim] - width, cells.shape[dim], axis=dim)
        cells = jnp.concatenate(
            [
                lax.ppermute(tail, axis, [(i, (i + 1) % count) for i in range(count)]),
                cells,
                lax.ppermute(head, axis, [((i + 1) % count, i) for i in range(count)]),
            ],
            axis=dim,
        )
    return cells


def profile(offset, spread):
    offsets = jnp.arange(-RADIUS, RADIUS + 1).astype(jnp.float32)
    norm_sum = jnp.sqrt(jnp.sum(jnp.exp(-offsets * offsets / (spread * spread))))
    inside = jnp.abs(offset) <= RADIUS
    return jnp.where(inside, jnp.exp(-offset * offset / (2.0 * spread * spread)), 0.0) / norm_sum


def band_pair(length, spread):
    rows_out = jnp.arange(length).astype(jnp.float32)[:, None]
    rows_in = jnp.arange(length + 2 * MARGIN).astype(jnp.float32)[None, :]
    offset = rows_out + MARGIN - rows_in
    smooth = profile(offset, spread)
    slope_part = -0.5 * (profile(offset + 1.0, spread) - profile(offset - 1.0, spread))
    return (smooth, slope_part)


def short_range(padded, size_x, size_y, size_z):
    mats_x = []
    mats_y = []
    mats_z = []
    for fraction, weight in zip(FRACTIONS, WEIGHTS):
        spread = RADIUS * fraction
        mats_x.append(jnp.stack(band_pair(size_x, spread)))
        mats_y.append(jnp.stack(band_pair(size_y, spread)))
        smooth_z, slope_z = band_pair(size_z, spread)
        mats_z.append(jnp.stack([weight * smooth_z, weight * slope_z]))
    stack_x = jnp.stack(mats_x)
    stack_y = jnp.stack(mats_y)
    stack_z = jnp.stack(mats_z)
    section_one = jnp.einsum("gsia,abc->gsibc", stack_x, padded, precision=PRECISE)
    section_two = jnp.einsum("gtjb,gibc->gtijc", stack_y, section_one[:, 0], precision=PRECISE)
    section_three = jnp.einsum(
        "gjb,gibc->gijc", stack_y[:, 0], section_one[:, 1], precision=PRECISE
    )
    smooth_pair = jnp.einsum("gijc,gtkc->tijk", section_two[:, 0], stack_z, precision=PRECISE)
    near_y = jnp.einsum("gijc,gkc->ijk", section_two[:, 1], stack_z[:, 0], precision=PRECISE)
    near_x = jnp.einsum("gijc,gkc->ijk", section_three, stack_z[:, 0], precision=PRECISE)
    return (smooth_pair[0], near_x, near_y, smooth_pair[1])


def unit_phase(product, modulus):
    angles = TWO_PI * (product % modulus).astype(jnp.float32) / modulus
    return (jnp.cos(angles), jnp.sin(angles))


def symbol(indices, length):
    angles = jnp.pi * indices.astype(jnp.float32) / length
    return (4.0 * jnp.sin(angles) ** 2, indices == length // 2, indices == 0)


def rotate(pattern, cos_t, sin_t, real_part, imag_part, direction):
    real_out = jnp.einsum(pattern, cos_t, real_part, precision=PRECISE) - direction * jnp.einsum(
        pattern, sin_t, imag_part, precision=PRECISE
    )
    imag_out = direction * jnp.einsum(pattern, sin_t, real_part, precision=PRECISE) + jnp.einsum(
        pattern, cos_t, imag_part, precision=PRECISE
    )
    return (real_out, imag_out)


def swap_rows(payload):
    return lax.all_to_all(payload, "gx", split_axis=2, concat_axis=2, tiled=True)


def swap_depth(payload):
    return lax.all_to_all(payload, "gz", split_axis=2, concat_axis=2, tiled=True)


def swap_columns(payload):
    return lax.all_to_all(payload, ("gx", "gy"), split_axis=2, concat_axis=2, tiled=True)


def long_range(density):
    size_x, size_y, size_z = density.shape
    count_gx = lax.axis_size("gx")
    count_gy = lax.axis_size("gy")
    count_gz = lax.axis_size("gz")
    local_x = size_x // 2
    local_y = size_y // 2
    local_z = size_z // 2
    depth_z = local_z // count_gx
    total_x = local_x * count_gz
    total_y = local_y * count_gx
    total_z = local_z * count_gy
    groups = count_gx * count_gy
    block_x = total_x // groups
    block_y = total_y // count_gz
    own_group = lax.axis_index("gx") * count_gy + lax.axis_index("gy")
    own_depth = lax.axis_index("gz")
    coarse = density.reshape(local_x, 2, local_y, 2, local_z, 2).mean(axis=(1, 3, 5))
    freq_y = jnp.arange(count_gz)[:, None] * block_y + jnp.arange(block_y)[None, :]
    pos_y = jnp.arange(count_gx)[:, None] * local_y + jnp.arange(local_y)[None, :]
    cos_y, sin_y = unit_phase(freq_y[:, :, None, None] * pos_y[None, None, :, :], total_y)
    rows_in = swap_rows(coarse.reshape(local_x, local_y, count_gx, depth_z))
    real_y = jnp.einsum("qrab,xbal->xqrl", cos_y, rows_in, precision=PRECISE)
    imag_y = -jnp.einsum("qrab,xbal->xqrl", sin_y, rows_in, precision=PRECISE)
    depth_in = swap_depth(jnp.stack([real_y, imag_y]))
    freq_x = jnp.arange(groups)[:, None] * block_x + jnp.arange(block_x)[None, :]
    pos_x = jnp.arange(count_gz)[:, None] * local_x + jnp.arange(local_x)[None, :]
    cos_x, sin_x = unit_phase(freq_x[:, :, None, None] * pos_x[None, None, :, :], total_x)
    real_x, imag_x = rotate("pscx,xcrl->sprl", cos_x, sin_x, depth_in[0], depth_in[1], -1.0)
    cols_in = swap_columns(jnp.stack([real_x, imag_x]))
    source = jnp.arange(groups)
    pos_z = (source % count_gy * local_z + source // count_gy * depth_z)[:, None] + jnp.arange(
        depth_z
    )[None, :]
    cos_z, sin_z = unit_phase(jnp.arange(total_z)[:, None, None] * pos_z[None, :, :], total_z)
    real_z, imag_z = rotate("kjl,sjrl->srk", cos_z, sin_z, cols_in[0], cols_in[1], -1.0)
    wave_x, edge_x, zero_x = symbol(own_group * block_x + jnp.arange(block_x), total_x)
    wave_y, edge_y, zero_y = symbol(own_depth * block_y + jnp.arange(block_y), total_y)
    wave_z, edge_z, zero_z = symbol(jnp.arange(total_z), total_z)
    kappa_sq = wave_x[:, None, None] + wave_y[None, :, None] + wave_z[None, None, :]
    dropped = edge_x[:, None, None] | edge_y[None, :, None] | edge_z[None, None, :]
    dropped = dropped | zero_x[:, None, None] & zero_y[None, :, None] & zero_z[None, None, :]
    green_fn = jnp.where(
        dropped,
        0.0,
        AMPLITUDE
        * jnp.exp(-SMOOTHING * SMOOTHING * kappa_sq)
        / (kappa_sq + 1.0 / (SCREEN * SCREEN)),
    )
    real_g = real_z * green_fn
    imag_g = imag_z * green_fn
    back_real, back_imag = rotate("kjl,srk->sjrl", cos_z, sin_z, real_g, imag_g, 1.0)
    cols_out = swap_columns(jnp.stack([back_real, back_imag]))
    real_b, imag_b = rotate("pscx,sprl->xcrl", cos_x, sin_x, cols_out[0], cols_out[1], 1.0)
    depth_out = swap_depth(jnp.stack([real_b, imag_b]))
    scale_y = jnp.ones(freq_y.shape, jnp.float32)
    result = jnp.einsum(
        "qrab,xqrl->xbal", cos_y * scale_y[:, :, None, None], depth_out[0], precision=PRECISE
    )
    result = result - jnp.einsum(
        "qrab,xqrl->xbal", sin_y * scale_y[:, :, None, None], depth_out[1], precision=PRECISE
    )
    result = result / (total_x * total_y * total_z)
    rows_out = swap_rows(result)
    return rows_out.reshape(local_x, local_y, local_z)


def transfer_pair(length):
    fine_cells = jnp.arange(-1, length + 1)
    parent = jnp.floor_divide(fine_cells, 2)
    parity = fine_cells - 2 * parent
    neighbour = parent - 1 + 2 * parity
    coarse_slots = jnp.arange(length // 2 + 2) - 1
    extended = 0.75 * (coarse_slots[None, :] == parent[:, None]).astype(jnp.float32)
    extended = extended + 0.25 * (coarse_slots[None, :] == neighbour[:, None]).astype(jnp.float32)
    value_map = extended[1 : length + 1]
    slope_map = -0.5 * (extended[2:] - extended[:-2])
    return (value_map, slope_map)


def prolong_brick(coarse_rims, size_x, size_y, size_z):
    value_x, slope_x = transfer_pair(size_x)
    value_y, slope_y = transfer_pair(size_y)
    value_z, slope_z = transfer_pair(size_z)
    along_z = jnp.einsum(
        "abe,tze->tabz", coarse_rims, jnp.stack([value_z, slope_z]), precision=PRECISE
    )
    level_y = jnp.einsum("aez,ye->ayz", along_z[0], value_y, precision=PRECISE)
    cross_y = jnp.einsum("aez,ye->ayz", along_z[0], slope_y, precision=PRECISE)
    cross_z = jnp.einsum("aez,ye->ayz", along_z[1], value_y, precision=PRECISE)
    far_pot = jnp.einsum("ayz,xa->xyz", level_y, value_x, precision=PRECISE)
    far_x = jnp.einsum("ayz,xa->xyz", level_y, slope_x, precision=PRECISE)
    far_y = jnp.einsum("ayz,xa->xyz", cross_y, value_x, precision=PRECISE)
    far_z = jnp.einsum("ayz,xa->xyz", cross_z, value_x, precision=PRECISE)
    return (far_pot, far_x, far_y, far_z)


def block_shards(density):
    size_x, size_y, size_z = density.shape
    padded = extended_2(density, (("gx", 1), ("gy", 2), ("gz", 0)), MARGIN)
    coarse_field = long_range(density)
    near_pot, near_x, near_y, near_z = short_range(padded, size_x, size_y, size_z)
    coarse_rims = extended_2(coarse_field, (("gx", 1), ("gy", 2), ("gz", 0)), 1)
    far_pot, far_x, far_y, far_z = prolong_brick(coarse_rims, size_x, size_y, size_z)
    potential = near_pot + far_pot
    forces = jnp.stack([near_x + far_x, near_y + far_y, near_z + far_z])
    return (potential, forces)


LANES = 128
ROWS = 8
NAMES = ("gx", "gy", "gz")


def cas(length):
    grid = np.outer(np.arange(length), np.arange(length)) % length
    angles = 2.0 * np.pi * grid / length
    return np.cos(angles) + np.sin(angles)


def averaging(length):
    out = np.zeros((length // 2, length))
    cells = np.arange(length // 2)
    out[cells, 2 * cells] = 0.5
    out[cells, 2 * cells + 1] = 0.5
    return out


def interpolation(length):
    half = length // 2
    out = np.zeros((length, half))
    cells = np.arange(half)
    out[2 * cells, cells] += 0.75
    out[2 * cells, (cells - 1) % half] += 0.25
    out[2 * cells + 1, cells] += 0.75
    out[2 * cells + 1, (cells + 1) % half] += 0.25
    return out


def slope_rows(values):
    return -0.5 * (np.roll(values, -1, 0) - np.roll(values, 1, 0))


def eigenvalues(length):
    offsets = np.arange(-RADIUS, RADIUS + 1)
    waves = np.cos(2.0 * np.pi * np.outer(np.arange(length), offsets) / length)
    out = []
    for fraction in FRACTIONS:
        spread = RADIUS * fraction
        norm = np.sqrt(np.sum(np.exp(-(offsets**2) / spread**2)))
        out.append(waves @ (np.exp(-(offsets**2) / (2.0 * spread**2)) / norm))
    return np.stack(out)


def green_table(sizes):
    waves = [4.0 * np.sin(np.pi * np.arange(m) / m) ** 2 for m in sizes]
    edges = [np.arange(m) == m // 2 for m in sizes]
    kappa = waves[0][:, None, None] + waves[1][None, :, None] + waves[2][None, None, :]
    dropped = edges[0][:, None, None] | edges[1][None, :, None] | edges[2][None, None, :]
    dropped[0, 0, 0] = True
    green = AMPLITUDE * np.exp(-SMOOTHING * SMOOTHING * kappa) / (kappa + 1.0 / SCREEN**2)
    return np.where(dropped, 0.0, green) / np.prod(sizes)


def tables(dims, count, halves, pair):
    nx, ny, nz = dims
    wide = nx // count
    hx, hy, hz = cas(nx), cas(ny), cas(nz)
    cx, cy, cz = cas(nx // 2), cas(ny // 2), cas(nz // 2)
    eye_h, eye_y, eye_k = np.eye(halves), np.eye(pair), np.eye(wide)
    side = halves * pair * nx
    out = {}
    out["hz"] = hz
    out["cz"] = (cz @ averaging(nz)).T
    out["lx"] = np.einsum("ab,yw,dkx->daykbwx", eye_h, eye_y, hx.reshape(count, wide, nx)).reshape(
        side, side
    )
    out["lxc"] = np.concatenate([cx @ averaging(nx) / pair] * pair, axis=1)
    out["ly"] = np.einsum("ab,kl,qsy->akqsbyl", eye_h, eye_k, hy.reshape(ny, count, pair)).reshape(
        side, side
    )
    out["lyc"] = cy
    fine = interpolation(ny) @ cy
    for name, level in (("value", hy), ("slope", slope_rows(hy))):
        out["by_" + name] = np.einsum(
            "ab,kl,syq->saykblq", eye_h, eye_k, level.reshape(count, pair, ny)
        ).reshape(side, side)
    level = np.zeros((count, ROWS, ny // 2))
    level[:, :pair] = fine.reshape(count, pair, -1)
    level[:, pair : 2 * pair] = slope_rows(fine).reshape(count, pair, -1)
    out["byc"] = level.reshape(count * ROWS, -1)
    out["bx"] = np.einsum("ab,yw,xdk->ayxdbwk", eye_h, eye_y, hx.reshape(nx, count, wide)).reshape(
        side, side
    )
    back = np.zeros((2 * pair, nx, count, ROWS))
    for row in range(2 * pair):
        back[row, :, :, row] = interpolation(nx) @ cx
    out["bxc"] = back.reshape(2 * pair * nx, count * ROWS)
    out["bzc"] = (interpolation(nz) @ cz).T
    ev_y, ev_z = eigenvalues(ny), eigenvalues(nz)
    weights = np.array(WEIGHTS) / (nx * ny * nz)
    plane = np.einsum("g,gy,gz->gyz", weights, ev_y, ev_z)
    out["plane"] = plane.reshape(len(WEIGHTS), ny, halves, LANES).transpose(0, 2, 1, 3)
    out["green"] = green_table((nx // 2, ny // 2, nz // 2))
    scalars = eigenvalues(nx).T.reshape(-1).astype(np.float32)
    return {k: np.asarray(v, np.float32) for k, v in out.items()}, scalars


def dot(a, b):
    return jnp.dot(a, b, precision=PRECISE, preferred_element_type=jnp.float32)


def spectral_kernel(shape, names, *refs):
    nx, ny, nz, gx, gy, gz = shape
    group, count = gy * gz, gx * gy * gz
    wide = nx // count
    n = len(names)
    data, scal = refs[0], refs[1]
    hbm = dict(zip(names, refs[2 : 2 + n]))
    out = refs[2 + n]
    tab = dict(zip(names, refs[3 + n : 3 + 2 * n]))
    (send_b, recv_a, recv_b, send_c, recv_c, send_d, recv_d, send_e, tab_sem, sems, semr) = refs[
        3 + 2 * n :
    ]
    ix, iy, iz = lax.axis_index("gx"), lax.axis_index("gy"), lax.axis_index("gz")
    mine = iz * gy + iy
    me = ix * group + mine

    def where(p):
        return {"gx": p // group, "gy": p % gy, "gz": (p % group) // gy}

    loads = {}
    for i, name in enumerate(names):
        source = hbm[name].at[me] if name == "green" else hbm[name]
        loads[name] = pltpu.make_async_copy(source, tab[name], tab_sem.at[i])
        loads[name].start()

    barrier = pltpu.get_barrier_semaphore()

    def greet(j, carry):
        pl.semaphore_signal(
            barrier, inc=1, device_id=where((me + j) % count), device_id_type=pl.DeviceIdType.MESH
        )
        return carry

    lax.fori_loop(1, count, greet, 0)
    pl.semaphore_wait(barrier, count - 1)

    def remote(src, dst, slot, p):
        return pltpu.make_async_remote_copy(
            src_ref=src,
            dst_ref=dst,
            send_sem=sems.at[slot],
            recv_sem=semr.at[slot],
            device_id=where(p),
            device_id_type=pl.DeviceIdType.MESH,
        )

    def group_exchange(base, source, target, own):
        def to(j):
            other = (mine + j) % group
            return remote(source(other), target(mine), base + j, ix * group + other)

        def arrived(j):
            other = (mine + group - j) % group
            return remote(source(other), target(other), base + j, ix * group + other)

        for j in range(1, group):
            to(j).start()
        own()
        for j in range(1, group):
            arrived(j).wait_recv()
        return lambda: [to(j).wait_send() for j in range(1, group)]

    def full_exchange(parts):
        def start(j, carry):
            other = (me + j) % count
            for base, source, target in parts:
                remote(source.at[other], target.at[me], base + j, other).start()
            return carry

        def arrive(j, carry):
            other = (me + count - j) % count
            for base, source, target in parts:
                remote(source.at[other], target.at[other], base + j, other).wait_recv()
            return carry

        def sent(j, carry):
            other = (me + j) % count
            for base, source, target in parts:
                remote(source.at[other], target.at[me], base + j, other).wait_send()
            return carry

        lax.fori_loop(1, count, start, 0)
        for base, source, target in parts:
            target[me] = source[me]
        lax.fori_loop(1, count, arrive, 0)
        lax.fori_loop(1, count, sent, 0)

    pair = recv_a.shape[1]
    edge = recv_a.shape[3]

    def keep_a():
        recv_a[iy, :, iz] = data[pl.ds(mine * pair, pair)]

    sent_a = group_exchange(
        0,
        lambda h: data.at[pl.ds(h * pair, pair)],
        lambda h: recv_a.at[h % gy, :, h // gy],
        keep_a,
    )
    for name in names:
        loads[name].wait()
    cells = jnp.concatenate(
        [recv_a[h].reshape(pair * nx, LANES) for h in range(gy)], axis=1
    )
    along = dot(cells, tab["hz"][...])
    along = jnp.concatenate([along[:, h * LANES : (h + 1) * LANES] for h in range(gy)], axis=0)
    send_b[...] = dot(tab["lx"][...], along).reshape(send_b.shape)
    send_c[:, 0, :] = dot(tab["lxc"][...], dot(cells, tab["cz"][...]))
    base = group
    full_exchange([(base, send_b, recv_b), (base + count, send_c, recv_c)])
    base += 2 * count
    spectrum = dot(tab["ly"][...], recv_b[...].reshape(count * ROWS, LANES))
    blocks = []
    for h in range(gy):
        for k in range(wide):
            row = h * wide + k
            response = sum(
                scal[(me * wide + k) * len(WEIGHTS) + g] * tab["plane"][g, h]
                for g in range(len(WEIGHTS))
            )
            blocks.append(spectrum[row * ny : (row + 1) * ny] * response)
    spectrum = jnp.concatenate(blocks, axis=0)
    coarse = dot(tab["lyc"][...], recv_c[:, 0, :]) * tab["green"][...]
    send_d[:, 0] = dot(tab["by_value"][...], spectrum).reshape(send_b.shape)
    send_d[:, 1] = dot(tab["by_slope"][...], spectrum).reshape(send_b.shape)
    send_d[:, 2] = dot(tab["byc"][...], coarse).reshape(send_b.shape)
    full_exchange([(base, send_d, recv_d)])
    base += count
    fields = []
    for f in range(2):
        level = dot(tab["bx"][...], recv_d[:, f].reshape(count * ROWS, LANES))
        size = pair * nx
        fields.append(
            jnp.concatenate([level[h * size : (h + 1) * size] for h in range(gy)], axis=1)
        )
    far = dot(tab["bxc"][...], recv_d[:, 2].reshape(count * ROWS, LANES))
    both = dot(jnp.concatenate(fields, axis=0), tab["hz"][...]) + dot(far, tab["bzc"][...])
    for y in range(pair):
        pot = both[y * nx : (y + 1) * nx]
        force_y = both[(pair + y) * nx : (pair + y + 1) * nx]
        force_x = -0.5 * (pltpu.roll(pot, nx - 1, 0) - pltpu.roll(pot, 1, 0))
        force_z = -0.5 * (pltpu.roll(pot, nz - 1, 1) - pltpu.roll(pot, 1, 1))
        for f, field in enumerate((pot, force_x, force_y, force_z)):
            for a in range(gz):
                for b in range(gy):
                    send_e[a * gy + b, f, y] = field[
                        a * edge : (a + 1) * edge, b * LANES : (b + 1) * LANES
                    ]

    def keep_e():
        out[:, pl.ds(mine * pair, pair)] = send_e[mine]

    sent_e = group_exchange(
        base,
        lambda h: send_e.at[h],
        lambda h: out.at[:, pl.ds(h * pair, pair)],
        keep_e,
    )
    sent_a()
    sent_e()


def spectral_fits(shape, counts):
    gx, gy, gz = counts
    nx, ny, nz = shape
    count = gx * gy * gz
    if ny % (2 * count) or ny != nx or nx != 2 * count or min(shape) < 2 * RADIUS + 2:
        return False
    return nz == 2 * LANES and gy == 2 and nx % (8 * gz) == 0


def spectral_shards(counts, density):
    gx, gy, gz = counts
    sx, sy, sz = density.shape
    dims = (sx * gz, sy * gx, sz * gy)
    count, group = gx * gy * gz, gy * gz
    pair = sy // group
    consts, scalars = tables(dims, count, gy, pair)
    names = tuple(consts)
    arrays = [consts[k] for k in names]
    any_spec = pl.BlockSpec(memory_space=pl.ANY)
    vmem = pl.BlockSpec(memory_space=pltpu.VMEM)
    tile = (count, ROWS, LANES)
    slots = 2 * group + 3 * count
    scratch = [
        pltpu.VMEM(a.shape[1:] if k == "green" else a.shape, jnp.float32)
        for k, a in consts.items()
    ]
    scratch += [
        pltpu.VMEM(tile, jnp.float32),
        pltpu.VMEM((gy, pair, gz, sx, LANES), jnp.float32),
        pltpu.VMEM(tile, jnp.float32),
        pltpu.VMEM((count, 1, LANES), jnp.float32),
        pltpu.VMEM((count, 1, LANES), jnp.float32),
        pltpu.VMEM((count, 3, ROWS, LANES), jnp.float32),
        pltpu.VMEM((count, 3, ROWS, LANES), jnp.float32),
        pltpu.VMEM((group, 4, pair, sx, LANES), jnp.float32),
        pltpu.SemaphoreType.DMA((len(names),)),
        pltpu.SemaphoreType.DMA((slots,)),
        pltpu.SemaphoreType.DMA((slots,)),
    ]
    fields = pl.pallas_call(
        functools.partial(spectral_kernel, dims + (gx, gy, gz), names),
        out_shape=jax.ShapeDtypeStruct((4, sy, sx, sz), jnp.float32),
        in_specs=[vmem, pl.BlockSpec(memory_space=pltpu.SMEM)] + [any_spec] * len(names),
        out_specs=vmem,
        scratch_shapes=scratch,
        compiler_params=pltpu.CompilerParams(collective_id=0, has_side_effects=True),
    )(density.transpose(1, 0, 2), jnp.asarray(scalars), *[jnp.asarray(a) for a in arrays])
    fields = fields.transpose(0, 2, 1, 3)
    return (fields[0], fields[1:])


def solution(mesh):
    counts = tuple(mesh.shape[a] for a in NAMES)

    def shards(density):
        sx, sy, sz = density.shape
        dims = (sx * counts[2], sy * counts[0], sz * counts[1])
        if spectral_fits(dims, counts):
            return spectral_shards(counts, density)
        return block_shards(density)

    return jax.shard_map(
        shards,
        mesh=mesh,
        in_specs=(P("gz", "gx", "gy"),),
        out_specs=(P("gz", "gx", "gy"), P(None, "gz", "gx", "gy")),
        check_vma=False,
    )
```

```python
import functools

import jax
import jax.numpy as jnp
import numpy as np
from jax import lax
from jax.experimental import pallas as pl
from jax.experimental.pallas import tpu as pltpu
from jax.sharding import PartitionSpec as P

RADIUS = 15
MARGIN = 16
SCREEN = 32


PRECISE = lax.Precision.HIGHEST
WEIGHTS = (1.0, 0.7, 0.5)
FRACTIONS = (0.5, 0.25, 0.125)
AMPLITUDE = 2.0
SMOOTHING = 1.0
TWO_PI = 6.283185307179586


def extended_2(cells, sides, width):
    for axis, dim in sides:
        count = lax.axis_size(axis)
        head = lax.slice_in_dim(cells, 0, width, axis=dim)
        tail = lax.slice_in_dim(cells, cells.shape[dim] - width, cells.shape[dim], axis=dim)
        cells = jnp.concatenate(
            [
                lax.ppermute(tail, axis, [(i, (i + 1) % count) for i in range(count)]),
                cells,
                lax.ppermute(head, axis, [((i + 1) % count, i) for i in range(count)]),
            ],
            axis=dim,
        )
    return cells


def profile(offset, spread):
    offsets = jnp.arange(-RADIUS, RADIUS + 1).astype(jnp.float32)
    norm_sum = jnp.sqrt(jnp.sum(jnp.exp(-offsets * offsets / (spread * spread))))
    inside = jnp.abs(offset) <= RADIUS
    return jnp.where(inside, jnp.exp(-offset * offset / (2.0 * spread * spread)), 0.0) / norm_sum


def band_pair(length, spread):
    rows_out = jnp.arange(length).astype(jnp.float32)[:, None]
    rows_in = jnp.arange(length + 2 * MARGIN).astype(jnp.float32)[None, :]
    offset = rows_out + MARGIN - rows_in
    smooth = profile(offset, spread)
    slope_part = -0.5 * (profile(offset + 1.0, spread) - profile(offset - 1.0, spread))
    return (smooth, slope_part)


def short_range(padded, size_x, size_y, size_z):
    mats_x = []
    mats_y = []
    mats_z = []
    for fraction, weight in zip(FRACTIONS, WEIGHTS):
        spread = RADIUS * fraction
        mats_x.append(jnp.stack(band_pair(size_x, spread)))
        mats_y.append(jnp.stack(band_pair(size_y, spread)))
        smooth_z, slope_z = band_pair(size_z, spread)
        mats_z.append(jnp.stack([weight * smooth_z, weight * slope_z]))
    stack_x = jnp.stack(mats_x)
    stack_y = jnp.stack(mats_y)
    stack_z = jnp.stack(mats_z)
    section_one = jnp.einsum("gsia,abc->gsibc", stack_x, padded, precision=PRECISE)
    section_two = jnp.einsum("gtjb,gibc->gtijc", stack_y, section_one[:, 0], precision=PRECISE)
    section_three = jnp.einsum(
        "gjb,gibc->gijc", stack_y[:, 0], section_one[:, 1], precision=PRECISE
    )
    smooth_pair = jnp.einsum("gijc,gtkc->tijk", section_two[:, 0], stack_z, precision=PRECISE)
    near_y = jnp.einsum("gijc,gkc->ijk", section_two[:, 1], stack_z[:, 0], precision=PRECISE)
    near_x = jnp.einsum("gijc,gkc->ijk", section_three, stack_z[:, 0], precision=PRECISE)
    return (smooth_pair[0], near_x, near_y, smooth_pair[1])


def unit_phase(product, modulus):
    angles = TWO_PI * (product % modulus).astype(jnp.float32) / modulus
    return (jnp.cos(angles), jnp.sin(angles))


def symbol(indices, length):
    angles = jnp.pi * indices.astype(jnp.float32) / length
    return (4.0 * jnp.sin(angles) ** 2, indices == length // 2, indices == 0)


def rotate(pattern, cos_t, sin_t, real_part, imag_part, direction):
    real_out = jnp.einsum(pattern, cos_t, real_part, precision=PRECISE) - direction * jnp.einsum(
        pattern, sin_t, imag_part, precision=PRECISE
    )
    imag_out = direction * jnp.einsum(pattern, sin_t, real_part, precision=PRECISE) + jnp.einsum(
        pattern, cos_t, imag_part, precision=PRECISE
    )
    return (real_out, imag_out)


def swap_rows(payload):
    return lax.all_to_all(payload, "gx", split_axis=2, concat_axis=2, tiled=True)


def swap_depth(payload):
    return lax.all_to_all(payload, "gz", split_axis=2, concat_axis=2, tiled=True)


def swap_columns(payload):
    return lax.all_to_all(payload, ("gx", "gy"), split_axis=2, concat_axis=2, tiled=True)


def long_range(density):
    size_x, size_y, size_z = density.shape
    count_gx = lax.axis_size("gx")
    count_gy = lax.axis_size("gy")
    count_gz = lax.axis_size("gz")
    local_x = size_x // 2
    local_y = size_y // 2
    local_z = size_z // 2
    depth_z = local_z // count_gx
    total_x = local_x * count_gz
    total_y = local_y * count_gx
    total_z = local_z * count_gy
    groups = count_gx * count_gy
    block_x = total_x // groups
    block_y = total_y // count_gz
    own_group = lax.axis_index("gx") * count_gy + lax.axis_index("gy")
    own_depth = lax.axis_index("gz")
    coarse = density.reshape(local_x, 2, local_y, 2, local_z, 2).mean(axis=(1, 3, 5))
    freq_y = jnp.arange(count_gz)[:, None] * block_y + jnp.arange(block_y)[None, :]
    pos_y = jnp.arange(count_gx)[:, None] * local_y + jnp.arange(local_y)[None, :]
    cos_y, sin_y = unit_phase(freq_y[:, :, None, None] * pos_y[None, None, :, :], total_y)
    rows_in = swap_rows(coarse.reshape(local_x, local_y, count_gx, depth_z))
    real_y = jnp.einsum("qrab,xbal->xqrl", cos_y, rows_in, precision=PRECISE)
    imag_y = -jnp.einsum("qrab,xbal->xqrl", sin_y, rows_in, precision=PRECISE)
    depth_in = swap_depth(jnp.stack([real_y, imag_y]))
    freq_x = jnp.arange(groups)[:, None] * block_x + jnp.arange(block_x)[None, :]
    pos_x = jnp.arange(count_gz)[:, None] * local_x + jnp.arange(local_x)[None, :]
    cos_x, sin_x = unit_phase(freq_x[:, :, None, None] * pos_x[None, None, :, :], total_x)
    real_x, imag_x = rotate("pscx,xcrl->sprl", cos_x, sin_x, depth_in[0], depth_in[1], -1.0)
    cols_in = swap_columns(jnp.stack([real_x, imag_x]))
    source = jnp.arange(groups)
    pos_z = (source % count_gy * local_z + source // count_gy * depth_z)[:, None] + jnp.arange(
        depth_z
    )[None, :]
    cos_z, sin_z = unit_phase(jnp.arange(total_z)[:, None, None] * pos_z[None, :, :], total_z)
    real_z, imag_z = rotate("kjl,sjrl->srk", cos_z, sin_z, cols_in[0], cols_in[1], -1.0)
    wave_x, edge_x, zero_x = symbol(own_group * block_x + jnp.arange(block_x), total_x)
    wave_y, edge_y, zero_y = symbol(own_depth * block_y + jnp.arange(block_y), total_y)
    wave_z, edge_z, zero_z = symbol(jnp.arange(total_z), total_z)
    kappa_sq = wave_x[:, None, None] + wave_y[None, :, None] + wave_z[None, None, :]
    dropped = edge_x[:, None, None] | edge_y[None, :, None] | edge_z[None, None, :]
    dropped = dropped | zero_x[:, None, None] & zero_y[None, :, None] & zero_z[None, None, :]
    green_fn = jnp.where(
        dropped,
        0.0,
        AMPLITUDE
        * jnp.exp(-SMOOTHING * SMOOTHING * kappa_sq)
        / (kappa_sq + 1.0 / (SCREEN * SCREEN)),
    )
    real_g = real_z * green_fn
    imag_g = imag_z * green_fn
    back_real, back_imag = rotate("kjl,srk->sjrl", cos_z, sin_z, real_g, imag_g, 1.0)
    cols_out = swap_columns(jnp.stack([back_real, back_imag]))
    real_b, imag_b = rotate("pscx,sprl->xcrl", cos_x, sin_x, cols_out[0], cols_out[1], 1.0)
    depth_out = swap_depth(jnp.stack([real_b, imag_b]))
    scale_y = jnp.ones(freq_y.shape, jnp.float32)
    result = jnp.einsum(
        "qrab,xqrl->xbal", cos_y * scale_y[:, :, None, None], depth_out[0], precision=PRECISE
    )
    result = result - jnp.einsum(
        "qrab,xqrl->xbal", sin_y * scale_y[:, :, None, None], depth_out[1], precision=PRECISE
    )
    result = result / (total_x * total_y * total_z)
    rows_out = swap_rows(result)
    return rows_out.reshape(local_x, local_y, local_z)


def transfer_pair(length):
    fine_cells = jnp.arange(-1, length + 1)
    parent = jnp.floor_divide(fine_cells, 2)
    parity = fine_cells - 2 * parent
    neighbour = parent - 1 + 2 * parity
    coarse_slots = jnp.arange(length // 2 + 2) - 1
    extended = 0.75 * (coarse_slots[None, :] == parent[:, None]).astype(jnp.float32)
    extended = extended + 0.25 * (coarse_slots[None, :] == neighbour[:, None]).astype(jnp.float32)
    value_map = extended[1 : length + 1]
    slope_map = -0.5 * (extended[2:] - extended[:-2])
    return (value_map, slope_map)


def prolong_brick(coarse_rims, size_x, size_y, size_z):
    value_x, slope_x = transfer_pair(size_x)
    value_y, slope_y = transfer_pair(size_y)
    value_z, slope_z = transfer_pair(size_z)
    along_z = jnp.einsum(
        "abe,tze->tabz", coarse_rims, jnp.stack([value_z, slope_z]), precision=PRECISE
    )
    level_y = jnp.einsum("aez,ye->ayz", along_z[0], value_y, precision=PRECISE)
    cross_y = jnp.einsum("aez,ye->ayz", along_z[0], slope_y, precision=PRECISE)
    cross_z = jnp.einsum("aez,ye->ayz", along_z[1], value_y, precision=PRECISE)
    far_pot = jnp.einsum("ayz,xa->xyz", level_y, value_x, precision=PRECISE)
    far_x = jnp.einsum("ayz,xa->xyz", level_y, slope_x, precision=PRECISE)
    far_y = jnp.einsum("ayz,xa->xyz", cross_y, value_x, precision=PRECISE)
    far_z = jnp.einsum("ayz,xa->xyz", cross_z, value_x, precision=PRECISE)
    return (far_pot, far_x, far_y, far_z)


def block_shards(density):
    size_x, size_y, size_z = density.shape
    padded = extended_2(density, (("gx", 1), ("gy", 2), ("gz", 0)), MARGIN)
    coarse_field = long_range(density)
    near_pot, near_x, near_y, near_z = short_range(padded, size_x, size_y, size_z)
    coarse_rims = extended_2(coarse_field, (("gx", 1), ("gy", 2), ("gz", 0)), 1)
    far_pot, far_x, far_y, far_z = prolong_brick(coarse_rims, size_x, size_y, size_z)
    potential = near_pot + far_pot
    forces = jnp.stack([near_x + far_x, near_y + far_y, near_z + far_z])
    return (potential, forces)


LANES = 128
ROWS = 8
NAMES = ("gx", "gy", "gz")


def cas(length):
    grid = np.outer(np.arange(length), np.arange(length)) % length
    angles = 2.0 * np.pi * grid / length
    return np.cos(angles) + np.sin(angles)


def averaging(length):
    out = np.zeros((length // 2, length))
    cells = np.arange(length // 2)
    out[cells, 2 * cells] = 0.5
    out[cells, 2 * cells + 1] = 0.5
    return out


def interpolation(length):
    half = length // 2
    out = np.zeros((length, half))
    cells = np.arange(half)
    out[2 * cells, cells] += 0.75
    out[2 * cells, (cells - 1) % half] += 0.25
    out[2 * cells + 1, cells] += 0.75
    out[2 * cells + 1, (cells + 1) % half] += 0.25
    return out


def slope_rows(values):
    return -0.5 * (np.roll(values, -1, 0) - np.roll(values, 1, 0))


def eigenvalues(length):
    offsets = np.arange(-RADIUS, RADIUS + 1)
    waves = np.cos(2.0 * np.pi * np.outer(np.arange(length), offsets) / length)
    out = []
    for fraction in FRACTIONS:
        spread = RADIUS * fraction
        norm = np.sqrt(np.sum(np.exp(-(offsets**2) / spread**2)))
        out.append(waves @ (np.exp(-(offsets**2) / (2.0 * spread**2)) / norm))
    return np.stack(out)


def green_table(sizes):
    waves = [4.0 * np.sin(np.pi * np.arange(m) / m) ** 2 for m in sizes]
    edges = [np.arange(m) == m // 2 for m in sizes]
    kappa = waves[0][:, None, None] + waves[1][None, :, None] + waves[2][None, None, :]
    dropped = edges[0][:, None, None] | edges[1][None, :, None] | edges[2][None, None, :]
    dropped[0, 0, 0] = True
    green = AMPLITUDE * np.exp(-SMOOTHING * SMOOTHING * kappa) / (kappa + 1.0 / SCREEN**2)
    return np.where(dropped, 0.0, green) / np.prod(sizes)


def tables(dims, count, halves, pair):
    nx, ny, nz = dims
    wide = nx // count
    hx, hy, hz = cas(nx), cas(ny), cas(nz)
    cx, cy, cz = cas(nx // 2), cas(ny // 2), cas(nz // 2)
    eye_h, eye_y, eye_k = np.eye(halves), np.eye(pair), np.eye(wide)
    side = halves * pair * nx
    out = {}
    out["hz"] = hz
    out["cz"] = (cz @ averaging(nz)).T
    out["lx"] = np.einsum("ab,yw,dkx->daykbwx", eye_h, eye_y, hx.reshape(count, wide, nx)).reshape(
        side, side
    )
    out["lxc"] = np.concatenate([cx @ averaging(nx) / pair] * pair, axis=1)
    out["ly"] = np.einsum("ab,kl,qsy->akqsbyl", eye_h, eye_k, hy.reshape(ny, count, pair)).reshape(
        side, side
    )
    out["lyc"] = cy
    fine = interpolation(ny) @ cy
    for name, level in (("value", hy), ("slope", slope_rows(hy))):
        out["by_" + name] = np.einsum(
            "ab,kl,syq->saykblq", eye_h, eye_k, level.reshape(count, pair, ny)
        ).reshape(side, side)
    level = np.zeros((count, ROWS, ny // 2))
    level[:, :pair] = fine.reshape(count, pair, -1)
    level[:, pair : 2 * pair] = slope_rows(fine).reshape(count, pair, -1)
    out["byc"] = level.reshape(count * ROWS, -1)
    out["bx"] = np.einsum("ab,yw,xdk->ayxdbwk", eye_h, eye_y, hx.reshape(nx, count, wide)).reshape(
        side, side
    )
    back = np.zeros((2 * pair, nx, count, ROWS))
    for row in range(2 * pair):
        back[row, :, :, row] = interpolation(nx) @ cx
    out["bxc"] = back.reshape(2 * pair * nx, count * ROWS)
    out["bzc"] = (interpolation(nz) @ cz).T
    ev_y, ev_z = eigenvalues(ny), eigenvalues(nz)
    weights = np.array(WEIGHTS) / (nx * ny * nz)
    plane = np.einsum("g,gy,gz->gyz", weights, ev_y, ev_z)
    out["plane"] = plane.reshape(len(WEIGHTS), ny, halves, LANES).transpose(0, 2, 1, 3)
    out["green"] = green_table((nx // 2, ny // 2, nz // 2))
    scalars = eigenvalues(nx).T.reshape(-1).astype(np.float32)
    return {k: np.asarray(v, np.float32) for k, v in out.items()}, scalars


def halves_of(values):
    high = values.astype(jnp.bfloat16)
    return high, (values - high.astype(jnp.float32)).astype(jnp.bfloat16)


SPLIT = ("hz", "cz", "lx", "lxc", "ly", "lyc", "by_value", "by_slope", "byc", "bx", "bxc", "bzc")


def dot(a, b):
    a_high, a_low = a if isinstance(a, tuple) else halves_of(a)
    b_high, b_low = b if isinstance(b, tuple) else halves_of(b)
    out = jnp.dot(a_high, b_low, preferred_element_type=jnp.float32)
    out = out + jnp.dot(a_low, b_high, preferred_element_type=jnp.float32)
    return out + jnp.dot(a_high, b_high, preferred_element_type=jnp.float32)


def spectral_kernel(shape, names, *refs):
    nx, ny, nz, gx, gy, gz = shape
    group, count = gy * gz, gx * gy * gz
    wide = nx // count
    n = len(names)
    data, scal = refs[0], refs[1]
    hbm = dict(zip(names, refs[2 : 2 + n]))
    out_pot, out_force = refs[2 + n : 4 + n]
    tab = dict(zip(names, refs[4 + n : 4 + 2 * n]))
    (
        turned,
        send_b,
        recv_a,
        recv_b,
        send_c,
        recv_c,
        send_d,
        recv_d,
        send_e,
        recv_e,
        tab_sem,
        sems,
        semr,
    ) = refs[4 + 2 * n :]
    ix, iy, iz = lax.axis_index("gx"), lax.axis_index("gy"), lax.axis_index("gz")
    mine = iz * gy + iy
    me = ix * group + mine
    pair = recv_a.shape[1]
    edge = recv_a.shape[3]

    def where(p):
        return {"gx": p // group, "gy": p % gy, "gz": (p % group) // gy}

    barrier = pltpu.get_barrier_semaphore()

    def greet(j, carry):
        pl.semaphore_signal(
            barrier, inc=1, device_id=where((me + j) % count), device_id_type=pl.DeviceIdType.MESH
        )
        return carry

    lax.fori_loop(1, count, greet, 0)

    loads = {}
    for i, name in enumerate(names):
        source = hbm[name].at[me] if name == "green" else hbm[name]
        loads[name] = pltpu.make_async_copy(source, tab[name], tab_sem.at[i])
        loads[name].start()

    def table(name):
        if name in loads:
            loads.pop(name).wait()
        values = tab[name]
        return (values[0], values[1]) if name in SPLIT else values

    turned[...] = jnp.transpose(data[...], (1, 0, 2))
    pl.semaphore_wait(barrier, count - 1)

    def remote(src, dst, slot, p):
        return pltpu.make_async_remote_copy(
            src_ref=src,
            dst_ref=dst,
            send_sem=sems.at[slot],
            recv_sem=semr.at[slot],
            device_id=where(p),
            device_id_type=pl.DeviceIdType.MESH,
        )

    def group_exchange(base, source, target):
        def to(j):
            other = (mine + j) % group
            return remote(source(other), target(mine), base + j, ix * group + other)

        def arrived(j):
            other = (mine + group - j) % group
            return remote(source(other), target(other), base + j, ix * group + other)

        for j in range(1, group):
            to(j).start()

        def arrive():
            for j in range(1, group):
                arrived(j).wait_recv()

        def sent():
            for j in range(1, group):
                to(j).wait_send()

        return arrive, sent

    def full_exchange(base, source, target):
        def start(j, carry):
            other = (me + j) % count
            remote(source(other), target(me), base + j, other).start()
            return carry

        def arrived(j, carry):
            other = (me + count - j) % count
            remote(source(other), target(other), base + j, other).wait_recv()
            return carry

        def gone(j, carry):
            other = (me + j) % count
            remote(source(other), target(me), base + j, other).wait_send()
            return carry

        lax.fori_loop(1, count, start, 0)
        return lambda: lax.fori_loop(1, count, arrived, 0), lambda: lax.fori_loop(1, count, gone, 0)

    pending = []
    arrive, sent = group_exchange(
        0,
        lambda h: turned.at[pl.ds(h * pair, pair)],
        lambda h: recv_a.at[h % gy, :, h // gy],
    )
    pending.append(sent)
    recv_a[iy, :, iz] = turned[pl.ds(mine * pair, pair)]
    hz, cz, lx, lxc = table("hz"), table("cz"), table("lx"), table("lxc")
    arrive()
    cells = halves_of(
        jnp.concatenate([recv_a[h].reshape(pair * nx, LANES) for h in range(gy)], axis=1)
    )
    along = dot(cells, hz)
    along = jnp.concatenate([along[:, h * LANES : (h + 1) * LANES] for h in range(gy)], axis=0)
    send_b[...] = dot(lx, along).reshape(send_b.shape)
    base = group
    arrive_b, sent = full_exchange(base, lambda p: send_b.at[p], lambda p: recv_b.at[p])
    pending.append(sent)
    send_c[:, 0, :] = dot(lxc, dot(cells, cz))
    base += count
    arrive_c, sent = full_exchange(base, lambda p: send_c.at[p], lambda p: recv_c.at[p])
    pending.append(sent)
    base += count
    recv_b[me] = send_b[me]
    recv_c[me] = send_c[me]
    plane = table("plane")
    responses = []
    for h in range(gy):
        for k in range(wide):
            responses.append(
                sum(
                    scal[(me * wide + k) * len(WEIGHTS) + g] * plane[g, h]
                    for g in range(len(WEIGHTS))
                )
            )
    response = jnp.concatenate(responses, axis=0)
    ly, lyc, green = table("ly"), table("lyc"), table("green")
    by_value, by_slope, byc = table("by_value"), table("by_slope"), table("byc")
    arrive_b()
    spectrum = dot(ly, recv_b[...].reshape(count * ROWS, LANES)) * response
    spectrum = halves_of(spectrum)
    send_d[:, 0] = dot(by_value, spectrum).reshape(send_b.shape)
    arrive_c()
    coarse = dot(lyc, recv_c[:, 0, :]) * green[...]
    send_d[:, 1] = dot(byc, coarse).reshape(send_b.shape)
    arrive_d, sent = full_exchange(
        base, lambda p: send_d.at[p, pl.ds(0, 2)], lambda p: recv_d.at[p, pl.ds(0, 2)]
    )
    pending.append(sent)
    base += count
    send_d[:, 2] = dot(by_slope, spectrum).reshape(send_b.shape)
    arrive_s, sent = full_exchange(base, lambda p: send_d.at[p, 2], lambda p: recv_d.at[p, 2])
    pending.append(sent)
    base += count
    recv_d[me] = send_d[me]
    bx, bxc, bzc = table("bx"), table("bxc"), table("bzc")
    size = pair * nx

    def near_part(f):
        level = dot(bx, recv_d[:, f].reshape(count * ROWS, LANES))
        level = jnp.concatenate([level[h * size : (h + 1) * size] for h in range(gy)], axis=1)
        return dot(level, hz)

    def place(f, y, field):
        for a in range(gz):
            for b in range(gy):
                send_e[a * gy + b, f, y] = field[
                    a * edge : (a + 1) * edge, b * LANES : (b + 1) * LANES
                ]

    arrive_d()
    far = dot(dot(bxc, recv_d[:, 1].reshape(count * ROWS, LANES)), bzc)
    values = near_part(0) + far[:size]
    for y in range(pair):
        pot = values[y * nx : (y + 1) * nx]
        place(0, y, pot)
        place(1, y, -0.5 * (pltpu.roll(pot, nx - 1, 0) - pltpu.roll(pot, 1, 0)))
        place(2, y, -0.5 * (pltpu.roll(pot, nz - 1, 1) - pltpu.roll(pot, 1, 1)))
    arrive_v, sent = group_exchange(
        base,
        lambda h: send_e.at[h, pl.ds(0, 3)],
        lambda h: recv_e.at[pl.ds(0, 3), pl.ds(h * pair, pair)],
    )
    pending.append(sent)
    base += group
    arrive_s()
    slopes = near_part(2) + far[size:]
    for y in range(pair):
        place(3, y, slopes[y * nx : (y + 1) * nx])
    arrive_y, sent = group_exchange(
        base,
        lambda h: send_e.at[h, 3],
        lambda h: recv_e.at[3, pl.ds(h * pair, pair)],
    )
    pending.append(sent)
    recv_e[:, pl.ds(mine * pair, pair)] = send_e[mine]
    arrive_v()
    out_pot[...] = jnp.transpose(recv_e[0], (1, 0, 2))
    out_force[0] = jnp.transpose(recv_e[1], (1, 0, 2))
    out_force[2] = jnp.transpose(recv_e[2], (1, 0, 2))
    arrive_y()
    out_force[1] = jnp.transpose(recv_e[3], (1, 0, 2))
    for sent in pending:
        sent()


def spectral_fits(shape, counts):
    gx, gy, gz = counts
    nx, ny, nz = shape
    count = gx * gy * gz
    if ny % (2 * count) or ny != nx or nx != 2 * count or min(shape) < 2 * RADIUS + 2:
        return False
    return nz == 2 * LANES and gy == 2 and nx % (8 * gz) == 0


def spectral_shards(counts, density):
    gx, gy, gz = counts
    sx, sy, sz = density.shape
    dims = (sx * gz, sy * gx, sz * gy)
    count, group = gx * gy * gz, gy * gz
    pair = sy // group
    consts, scalars = tables(dims, count, gy, pair)
    names = tuple(consts)
    for name in SPLIT:
        full = consts[name]
        high = full.astype(jnp.bfloat16)
        consts[name] = np.stack([high, (full - high.astype(np.float32)).astype(jnp.bfloat16)])
    arrays = [consts[k] for k in names]
    any_spec = pl.BlockSpec(memory_space=pl.ANY)
    vmem = pl.BlockSpec(memory_space=pltpu.VMEM)
    tile = (count, ROWS, LANES)
    slots = 3 * group + 4 * count
    scratch = [
        pltpu.VMEM(a.shape[1:] if k == "green" else a.shape, a.dtype)
        for k, a in consts.items()
    ]
    scratch += [
        pltpu.VMEM((sy, sx, sz), jnp.float32),
        pltpu.VMEM(tile, jnp.float32),
        pltpu.VMEM((gy, pair, gz, sx, LANES), jnp.float32),
        pltpu.VMEM(tile, jnp.float32),
        pltpu.VMEM((count, 1, LANES), jnp.float32),
        pltpu.VMEM((count, 1, LANES), jnp.float32),
        pltpu.VMEM((count, 3, ROWS, LANES), jnp.float32),
        pltpu.VMEM((count, 3, ROWS, LANES), jnp.float32),
        pltpu.VMEM((group, 4, pair, sx, LANES), jnp.float32),
        pltpu.VMEM((4, sy, sx, LANES), jnp.float32),
        pltpu.SemaphoreType.DMA((len(names),)),
        pltpu.SemaphoreType.DMA((slots,)),
        pltpu.SemaphoreType.DMA((slots,)),
    ]
    return pl.pallas_call(
        functools.partial(spectral_kernel, dims + (gx, gy, gz), names),
        out_shape=(
            jax.ShapeDtypeStruct((sx, sy, sz), jnp.float32),
            jax.ShapeDtypeStruct((3, sx, sy, sz), jnp.float32),
        ),
        in_specs=[vmem, pl.BlockSpec(memory_space=pltpu.SMEM)] + [any_spec] * len(names),
        out_specs=(vmem, vmem),
        scratch_shapes=scratch,
        compiler_params=pltpu.CompilerParams(collective_id=0, has_side_effects=True),
    )(density, jnp.asarray(scalars), *[jnp.asarray(a) for a in arrays])


def solution(mesh):
    counts = tuple(mesh.shape[a] for a in NAMES)

    def shards(density):
        sx, sy, sz = density.shape
        dims = (sx * counts[2], sy * counts[0], sz * counts[1])
        if spectral_fits(dims, counts):
            return spectral_shards(counts, density)
        return block_shards(density)

    return jax.shard_map(
        shards,
        mesh=mesh,
        in_specs=(P("gz", "gx", "gy"),),
        out_specs=(P("gz", "gx", "gy"), P(None, "gz", "gx", "gy")),
        check_vma=False,
    )
```

```python
import functools

import jax
import jax.numpy as jnp
import numpy as np
from jax import lax
from jax.experimental import pallas as pl
from jax.experimental.pallas import tpu as pltpu
from jax.sharding import PartitionSpec as P

RADIUS = 15
MARGIN = 16
SCREEN = 32


PRECISE = lax.Precision.HIGHEST
WEIGHTS = (1.0, 0.7, 0.5)
FRACTIONS = (0.5, 0.25, 0.125)
AMPLITUDE = 2.0
SMOOTHING = 1.0
TWO_PI = 6.283185307179586


def extended_2(cells, sides, width):
    for axis, dim in sides:
        count = lax.axis_size(axis)
        head = lax.slice_in_dim(cells, 0, width, axis=dim)
        tail = lax.slice_in_dim(cells, cells.shape[dim] - width, cells.shape[dim], axis=dim)
        cells = jnp.concatenate(
            [
                lax.ppermute(tail, axis, [(i, (i + 1) % count) for i in range(count)]),
                cells,
                lax.ppermute(head, axis, [((i + 1) % count, i) for i in range(count)]),
            ],
            axis=dim,
        )
    return cells


def profile(offset, spread):
    offsets = jnp.arange(-RADIUS, RADIUS + 1).astype(jnp.float32)
    norm_sum = jnp.sqrt(jnp.sum(jnp.exp(-offsets * offsets / (spread * spread))))
    inside = jnp.abs(offset) <= RADIUS
    return jnp.where(inside, jnp.exp(-offset * offset / (2.0 * spread * spread)), 0.0) / norm_sum


def band_pair(length, spread):
    rows_out = jnp.arange(length).astype(jnp.float32)[:, None]
    rows_in = jnp.arange(length + 2 * MARGIN).astype(jnp.float32)[None, :]
    offset = rows_out + MARGIN - rows_in
    smooth = profile(offset, spread)
    slope_part = -0.5 * (profile(offset + 1.0, spread) - profile(offset - 1.0, spread))
    return (smooth, slope_part)


def short_range(padded, size_x, size_y, size_z):
    mats_x = []
    mats_y = []
    mats_z = []
    for fraction, weight in zip(FRACTIONS, WEIGHTS):
        spread = RADIUS * fraction
        mats_x.append(jnp.stack(band_pair(size_x, spread)))
        mats_y.append(jnp.stack(band_pair(size_y, spread)))
        smooth_z, slope_z = band_pair(size_z, spread)
        mats_z.append(jnp.stack([weight * smooth_z, weight * slope_z]))
    stack_x = jnp.stack(mats_x)
    stack_y = jnp.stack(mats_y)
    stack_z = jnp.stack(mats_z)
    section_one = jnp.einsum("gsia,abc->gsibc", stack_x, padded, precision=PRECISE)
    section_two = jnp.einsum("gtjb,gibc->gtijc", stack_y, section_one[:, 0], precision=PRECISE)
    section_three = jnp.einsum(
        "gjb,gibc->gijc", stack_y[:, 0], section_one[:, 1], precision=PRECISE
    )
    smooth_pair = jnp.einsum("gijc,gtkc->tijk", section_two[:, 0], stack_z, precision=PRECISE)
    near_y = jnp.einsum("gijc,gkc->ijk", section_two[:, 1], stack_z[:, 0], precision=PRECISE)
    near_x = jnp.einsum("gijc,gkc->ijk", section_three, stack_z[:, 0], precision=PRECISE)
    return (smooth_pair[0], near_x, near_y, smooth_pair[1])


def unit_phase(product, modulus):
    angles = TWO_PI * (product % modulus).astype(jnp.float32) / modulus
    return (jnp.cos(angles), jnp.sin(angles))


def symbol(indices, length):
    angles = jnp.pi * indices.astype(jnp.float32) / length
    return (4.0 * jnp.sin(angles) ** 2, indices == length // 2, indices == 0)


def rotate(pattern, cos_t, sin_t, real_part, imag_part, direction):
    real_out = jnp.einsum(pattern, cos_t, real_part, precision=PRECISE) - direction * jnp.einsum(
        pattern, sin_t, imag_part, precision=PRECISE
    )
    imag_out = direction * jnp.einsum(pattern, sin_t, real_part, precision=PRECISE) + jnp.einsum(
        pattern, cos_t, imag_part, precision=PRECISE
    )
    return (real_out, imag_out)


def swap_rows(payload):
    return lax.all_to_all(payload, "gx", split_axis=2, concat_axis=2, tiled=True)


def swap_depth(payload):
    return lax.all_to_all(payload, "gz", split_axis=2, concat_axis=2, tiled=True)


def swap_columns(payload):
    return lax.all_to_all(payload, ("gx", "gy"), split_axis=2, concat_axis=2, tiled=True)


def long_range(density):
    size_x, size_y, size_z = density.shape
    count_gx = lax.axis_size("gx")
    count_gy = lax.axis_size("gy")
    count_gz = lax.axis_size("gz")
    local_x = size_x // 2
    local_y = size_y // 2
    local_z = size_z // 2
    depth_z = local_z // count_gx
    total_x = local_x * count_gz
    total_y = local_y * count_gx
    total_z = local_z * count_gy
    groups = count_gx * count_gy
    block_x = total_x // groups
    block_y = total_y // count_gz
    own_group = lax.axis_index("gx") * count_gy + lax.axis_index("gy")
    own_depth = lax.axis_index("gz")
    coarse = density.reshape(local_x, 2, local_y, 2, local_z, 2).mean(axis=(1, 3, 5))
    freq_y = jnp.arange(count_gz)[:, None] * block_y + jnp.arange(block_y)[None, :]
    pos_y = jnp.arange(count_gx)[:, None] * local_y + jnp.arange(local_y)[None, :]
    cos_y, sin_y = unit_phase(freq_y[:, :, None, None] * pos_y[None, None, :, :], total_y)
    rows_in = swap_rows(coarse.reshape(local_x, local_y, count_gx, depth_z))
    real_y = jnp.einsum("qrab,xbal->xqrl", cos_y, rows_in, precision=PRECISE)
    imag_y = -jnp.einsum("qrab,xbal->xqrl", sin_y, rows_in, precision=PRECISE)
    depth_in = swap_depth(jnp.stack([real_y, imag_y]))
    freq_x = jnp.arange(groups)[:, None] * block_x + jnp.arange(block_x)[None, :]
    pos_x = jnp.arange(count_gz)[:, None] * local_x + jnp.arange(local_x)[None, :]
    cos_x, sin_x = unit_phase(freq_x[:, :, None, None] * pos_x[None, None, :, :], total_x)
    real_x, imag_x = rotate("pscx,xcrl->sprl", cos_x, sin_x, depth_in[0], depth_in[1], -1.0)
    cols_in = swap_columns(jnp.stack([real_x, imag_x]))
    source = jnp.arange(groups)
    pos_z = (source % count_gy * local_z + source // count_gy * depth_z)[:, None] + jnp.arange(
        depth_z
    )[None, :]
    cos_z, sin_z = unit_phase(jnp.arange(total_z)[:, None, None] * pos_z[None, :, :], total_z)
    real_z, imag_z = rotate("kjl,sjrl->srk", cos_z, sin_z, cols_in[0], cols_in[1], -1.0)
    wave_x, edge_x, zero_x = symbol(own_group * block_x + jnp.arange(block_x), total_x)
    wave_y, edge_y, zero_y = symbol(own_depth * block_y + jnp.arange(block_y), total_y)
    wave_z, edge_z, zero_z = symbol(jnp.arange(total_z), total_z)
    kappa_sq = wave_x[:, None, None] + wave_y[None, :, None] + wave_z[None, None, :]
    dropped = edge_x[:, None, None] | edge_y[None, :, None] | edge_z[None, None, :]
    dropped = dropped | zero_x[:, None, None] & zero_y[None, :, None] & zero_z[None, None, :]
    green_fn = jnp.where(
        dropped,
        0.0,
        AMPLITUDE
        * jnp.exp(-SMOOTHING * SMOOTHING * kappa_sq)
        / (kappa_sq + 1.0 / (SCREEN * SCREEN)),
    )
    real_g = real_z * green_fn
    imag_g = imag_z * green_fn
    back_real, back_imag = rotate("kjl,srk->sjrl", cos_z, sin_z, real_g, imag_g, 1.0)
    cols_out = swap_columns(jnp.stack([back_real, back_imag]))
    real_b, imag_b = rotate("pscx,sprl->xcrl", cos_x, sin_x, cols_out[0], cols_out[1], 1.0)
    depth_out = swap_depth(jnp.stack([real_b, imag_b]))
    scale_y = jnp.ones(freq_y.shape, jnp.float32)
    result = jnp.einsum(
        "qrab,xqrl->xbal", cos_y * scale_y[:, :, None, None], depth_out[0], precision=PRECISE
    )
    result = result - jnp.einsum(
        "qrab,xqrl->xbal", sin_y * scale_y[:, :, None, None], depth_out[1], precision=PRECISE
    )
    result = result / (total_x * total_y * total_z)
    rows_out = swap_rows(result)
    return rows_out.reshape(local_x, local_y, local_z)


def transfer_pair(length):
    fine_cells = jnp.arange(-1, length + 1)
    parent = jnp.floor_divide(fine_cells, 2)
    parity = fine_cells - 2 * parent
    neighbour = parent - 1 + 2 * parity
    coarse_slots = jnp.arange(length // 2 + 2) - 1
    extended = 0.75 * (coarse_slots[None, :] == parent[:, None]).astype(jnp.float32)
    extended = extended + 0.25 * (coarse_slots[None, :] == neighbour[:, None]).astype(jnp.float32)
    value_map = extended[1 : length + 1]
    slope_map = -0.5 * (extended[2:] - extended[:-2])
    return (value_map, slope_map)


def prolong_brick(coarse_rims, size_x, size_y, size_z):
    value_x, slope_x = transfer_pair(size_x)
    value_y, slope_y = transfer_pair(size_y)
    value_z, slope_z = transfer_pair(size_z)
    along_z = jnp.einsum(
        "abe,tze->tabz", coarse_rims, jnp.stack([value_z, slope_z]), precision=PRECISE
    )
    level_y = jnp.einsum("aez,ye->ayz", along_z[0], value_y, precision=PRECISE)
    cross_y = jnp.einsum("aez,ye->ayz", along_z[0], slope_y, precision=PRECISE)
    cross_z = jnp.einsum("aez,ye->ayz", along_z[1], value_y, precision=PRECISE)
    far_pot = jnp.einsum("ayz,xa->xyz", level_y, value_x, precision=PRECISE)
    far_x = jnp.einsum("ayz,xa->xyz", level_y, slope_x, precision=PRECISE)
    far_y = jnp.einsum("ayz,xa->xyz", cross_y, value_x, precision=PRECISE)
    far_z = jnp.einsum("ayz,xa->xyz", cross_z, value_x, precision=PRECISE)
    return (far_pot, far_x, far_y, far_z)


def block_shards(density):
    size_x, size_y, size_z = density.shape
    padded = extended_2(density, (("gx", 1), ("gy", 2), ("gz", 0)), MARGIN)
    coarse_field = long_range(density)
    near_pot, near_x, near_y, near_z = short_range(padded, size_x, size_y, size_z)
    coarse_rims = extended_2(coarse_field, (("gx", 1), ("gy", 2), ("gz", 0)), 1)
    far_pot, far_x, far_y, far_z = prolong_brick(coarse_rims, size_x, size_y, size_z)
    potential = near_pot + far_pot
    forces = jnp.stack([near_x + far_x, near_y + far_y, near_z + far_z])
    return (potential, forces)


LANES = 128
ROWS = 8
NAMES = ("gx", "gy", "gz")


def cas(length):
    grid = np.outer(np.arange(length), np.arange(length)) % length
    angles = 2.0 * np.pi * grid / length
    return np.cos(angles) + np.sin(angles)


def averaging(length):
    out = np.zeros((length // 2, length))
    cells = np.arange(length // 2)
    out[cells, 2 * cells] = 0.5
    out[cells, 2 * cells + 1] = 0.5
    return out


def interpolation(length):
    half = length // 2
    out = np.zeros((length, half))
    cells = np.arange(half)
    out[2 * cells, cells] += 0.75
    out[2 * cells, (cells - 1) % half] += 0.25
    out[2 * cells + 1, cells] += 0.75
    out[2 * cells + 1, (cells + 1) % half] += 0.25
    return out


def slope_rows(values):
    return -0.5 * (np.roll(values, -1, 0) - np.roll(values, 1, 0))


def eigenvalues(length):
    offsets = np.arange(-RADIUS, RADIUS + 1)
    waves = np.cos(2.0 * np.pi * np.outer(np.arange(length), offsets) / length)
    out = []
    for fraction in FRACTIONS:
        spread = RADIUS * fraction
        norm = np.sqrt(np.sum(np.exp(-(offsets**2) / spread**2)))
        out.append(waves @ (np.exp(-(offsets**2) / (2.0 * spread**2)) / norm))
    return np.stack(out)


def green_table(sizes):
    waves = [4.0 * np.sin(np.pi * np.arange(m) / m) ** 2 for m in sizes]
    edges = [np.arange(m) == m // 2 for m in sizes]
    kappa = waves[0][:, None, None] + waves[1][None, :, None] + waves[2][None, None, :]
    dropped = edges[0][:, None, None] | edges[1][None, :, None] | edges[2][None, None, :]
    dropped[0, 0, 0] = True
    green = AMPLITUDE * np.exp(-SMOOTHING * SMOOTHING * kappa) / (kappa + 1.0 / SCREEN**2)
    return np.where(dropped, 0.0, green) / np.prod(sizes)


def tables(dims, count, halves, pair):
    nx, ny, nz = dims
    wide = nx // count
    hx, hy, hz = cas(nx), cas(ny), cas(nz)
    cx, cy, cz = cas(nx // 2), cas(ny // 2), cas(nz // 2)
    eye_h, eye_y, eye_k = np.eye(halves), np.eye(pair), np.eye(wide)
    side = halves * pair * nx
    out = {}
    out["hz"] = hz
    out["cz"] = (cz @ averaging(nz)).T
    out["lx"] = np.einsum("ab,yw,dkx->daykbwx", eye_h, eye_y, hx.reshape(count, wide, nx)).reshape(
        side, side
    )
    out["lxc"] = np.concatenate([cx @ averaging(nx) / pair] * pair, axis=1)
    out["ly"] = np.einsum("ab,kl,qsy->akqsbyl", eye_h, eye_k, hy.reshape(ny, count, pair)).reshape(
        side, side
    )
    out["lyc"] = cy
    fine = interpolation(ny) @ cy
    for name, level in (("value", hy), ("slope", slope_rows(hy))):
        out["by_" + name] = np.einsum(
            "ab,kl,syq->saykblq", eye_h, eye_k, level.reshape(count, pair, ny)
        ).reshape(side, side)
    level = np.zeros((count, ROWS, ny // 2))
    level[:, :pair] = fine.reshape(count, pair, -1)
    level[:, pair : 2 * pair] = slope_rows(fine).reshape(count, pair, -1)
    out["byc"] = level.reshape(count * ROWS, -1)
    out["bx"] = np.einsum("ab,yw,xdk->ayxdbwk", eye_h, eye_y, hx.reshape(nx, count, wide)).reshape(
        side, side
    )
    back = np.zeros((2 * pair, nx, count, ROWS))
    for row in range(2 * pair):
        back[row, :, :, row] = interpolation(nx) @ cx
    out["bxc"] = back.reshape(2 * pair * nx, count * ROWS)
    out["bzc"] = (interpolation(nz) @ cz).T
    ev_y, ev_z = eigenvalues(ny), eigenvalues(nz)
    weights = np.array(WEIGHTS) / (nx * ny * nz)
    plane = np.einsum("g,gy,gz->gyz", weights, ev_y, ev_z)
    out["plane"] = plane.reshape(len(WEIGHTS), ny, halves, LANES).transpose(0, 2, 1, 3)
    out["green"] = green_table((nx // 2, ny // 2, nz // 2))
    scalars = eigenvalues(nx).T.reshape(-1).astype(np.float32)
    return {k: np.asarray(v, np.float32) for k, v in out.items()}, scalars


def halves_of(values):
    high = values.astype(jnp.bfloat16)
    return high, (values - high.astype(jnp.float32)).astype(jnp.bfloat16)


SPLIT = ("hz", "cz", "lx", "lxc", "ly", "lyc", "by_value", "by_slope", "byc", "bx", "bxc", "bzc")


def dot(a, b):
    a_high, a_low = a if isinstance(a, tuple) else halves_of(a)
    b_high, b_low = b if isinstance(b, tuple) else halves_of(b)
    out = jnp.dot(a_high, b_low, preferred_element_type=jnp.float32)
    out = out + jnp.dot(a_low, b_high, preferred_element_type=jnp.float32)
    return out + jnp.dot(a_high, b_high, preferred_element_type=jnp.float32)


def spectral_kernel(shape, names, *refs):
    nx, ny, nz, gx, gy, gz = shape
    group, count = gy * gz, gx * gy * gz
    wide = nx // count
    n = len(names)
    hbm = dict(zip(names, refs[:n]))
    recv_e = refs[n]
    tab = dict(zip(names, refs[n + 1 : 2 * n + 1]))
    (
        turned,
        send_b,
        recv_a,
        recv_b,
        send_c,
        recv_c,
        send_d,
        recv_d,
        send_s,
        recv_s,
        send_e,
        tab_sem,
        sems,
        semr,
    ) = refs[2 * n + 1 :]
    ix, iy, iz = lax.axis_index("gx"), lax.axis_index("gy"), lax.axis_index("gz")
    mine = iz * gy + iy
    me = ix * group + mine
    pair = recv_a.shape[1]
    edge = recv_a.shape[3]

    def where(p):
        return {"gx": p // group, "gy": p % gy, "gz": (p % group) // gy}

    barrier = pltpu.get_barrier_semaphore()

    def greet(j, carry):
        pl.semaphore_signal(
            barrier, inc=1, device_id=where((me + j) % count), device_id_type=pl.DeviceIdType.MESH
        )
        return carry

    lax.fori_loop(1, count, greet, 0, unroll=True)

    loads = {}
    for i, name in enumerate(names):
        source = hbm[name].at[me] if name == "green" else hbm[name]
        loads[name] = pltpu.make_async_copy(source, tab[name], tab_sem.at[i])
        loads[name].start()

    def table(name):
        if name in loads:
            loads.pop(name).wait()
        values = tab[name]
        return (values[0], values[1]) if name in SPLIT else values

    scal = tab["scalars"]
    turned[...] = jnp.transpose(table("density")[...], (1, 0, 2))
    pl.semaphore_wait(barrier, count - 1)

    def remote(src, dst, slot, p):
        return pltpu.make_async_remote_copy(
            src_ref=src,
            dst_ref=dst,
            send_sem=sems.at[slot],
            recv_sem=semr.at[slot],
            device_id=where(p),
            device_id_type=pl.DeviceIdType.MESH,
        )

    def group_exchange(slot, source, target, some_source, some_target):
        for j in range(1, group):
            other = (mine + j) % group
            remote(source(other), target(mine), slot, ix * group + other).start()
        total = remote(some_source, some_target, slot, ix * group + (mine + 1) % group)
        return total.wait_recv, total.wait_send

    def full_exchange(slot, source, target):
        def start(j, carry):
            other = (me + j) % count
            remote(source.at[other], target.at[me], slot, other).start()
            return carry

        lax.fori_loop(1, count, start, 0, unroll=True)
        rest = pl.ds(0, count - 1)
        total = remote(source.at[rest], target.at[rest], slot, (me + 1) % count)
        return total.wait_recv, total.wait_send

    pending = []
    arrive, sent = group_exchange(
        0,
        lambda h: turned.at[pl.ds(h * pair, pair)],
        lambda h: recv_a.at[h % gy, :, h // gy],
        turned.at[pl.ds(0, (group - 1) * pair)],
        turned.at[pl.ds(0, (group - 1) * pair)],
    )
    pending.append(sent)
    recv_a[iy, :, iz] = turned[pl.ds(mine * pair, pair)]
    hz, cz, lx, lxc = table("hz"), table("cz"), table("lx"), table("lxc")
    arrive()
    cells = halves_of(
        jnp.concatenate([recv_a[h].reshape(pair * nx, LANES) for h in range(gy)], axis=1)
    )
    along = dot(cells, hz)
    along = jnp.concatenate([along[:, h * LANES : (h + 1) * LANES] for h in range(gy)], axis=0)
    send_b[...] = dot(lx, along).reshape(send_b.shape)
    arrive_b, sent = full_exchange(1, send_b, recv_b)
    pending.append(sent)
    send_c[:, 0, :] = dot(lxc, dot(cells, cz))
    arrive_c, sent = full_exchange(2, send_c, recv_c)
    pending.append(sent)
    recv_b[me] = send_b[me]
    recv_c[me] = send_c[me]
    table("scalars")
    plane = table("plane")
    responses = []
    for h in range(gy):
        for k in range(wide):
            responses.append(
                sum(
                    scal[(me * wide + k) * len(WEIGHTS) + g] * plane[g, h]
                    for g in range(len(WEIGHTS))
                )
            )
    response = jnp.concatenate(responses, axis=0)
    ly, lyc, green = table("ly"), table("lyc"), table("green")
    by_value, by_slope, byc = table("by_value"), table("by_slope"), table("byc")
    arrive_b()
    spectrum = dot(ly, recv_b[...].reshape(count * ROWS, LANES)) * response
    spectrum = halves_of(spectrum)
    send_d[:, 0] = dot(by_value, spectrum).reshape(send_b.shape)
    arrive_c()
    coarse = dot(lyc, recv_c[:, 0, :]) * green[...]
    send_d[:, 1] = dot(byc, coarse).reshape(send_b.shape)
    arrive_d, sent = full_exchange(3, send_d, recv_d)
    pending.append(sent)
    send_s[...] = dot(by_slope, spectrum).reshape(send_b.shape)
    arrive_s, sent = full_exchange(4, send_s, recv_s)
    pending.append(sent)
    recv_d[me] = send_d[me]
    recv_s[me] = send_s[me]
    bx, bxc, bzc = table("bx"), table("bxc"), table("bzc")
    size = pair * nx

    def near_part(received):
        level = dot(bx, received.reshape(count * ROWS, LANES))
        level = jnp.concatenate([level[h * size : (h + 1) * size] for h in range(gy)], axis=1)
        return dot(level, hz)

    def place(f, y, field):
        for a in range(gz):
            for b in range(gy):
                send_e[a * gy + b, f, y] = field[
                    a * edge : (a + 1) * edge, b * LANES : (b + 1) * LANES
                ]

    arrive_d()
    far = dot(dot(bxc, recv_d[:, 1].reshape(count * ROWS, LANES)), bzc)
    values = near_part(recv_d[:, 0]) + far[:size]
    for y in range(pair):
        pot = values[y * nx : (y + 1) * nx]
        place(0, y, pot)
        place(1, y, -0.5 * (pltpu.roll(pot, nx - 1, 0) - pltpu.roll(pot, 1, 0)))
        place(2, y, -0.5 * (pltpu.roll(pot, nz - 1, 1) - pltpu.roll(pot, 1, 1)))
    arrive_v, sent = group_exchange(
        5,
        lambda h: send_e.at[h, pl.ds(0, 3)],
        lambda h: recv_e.at[pl.ds(0, 3), pl.ds(h * pair, pair)],
        send_e.at[pl.ds(0, group - 1), pl.ds(0, 3)],
        send_e.at[pl.ds(0, group - 1), pl.ds(0, 3)],
    )
    pending.append(sent)
    arrive_s()
    slopes = near_part(recv_s[...]) + far[size:]
    for y in range(pair):
        place(3, y, slopes[y * nx : (y + 1) * nx])
    arrive_y, sent = group_exchange(
        6,
        lambda h: send_e.at[h, 3],
        lambda h: recv_e.at[3, pl.ds(h * pair, pair)],
        send_e.at[pl.ds(0, group - 1), 3],
        send_e.at[pl.ds(0, group - 1), 3],
    )
    pending.append(sent)
    recv_e[:, pl.ds(mine * pair, pair)] = send_e[mine]
    arrive_v()
    arrive_y()
    for sent in pending:
        sent()


def hand_out(fields, out_pot, out_force):
    out_pot[...] = jnp.transpose(fields[0], (1, 0, 2))
    out_force[0] = jnp.transpose(fields[1], (1, 0, 2))
    out_force[1] = jnp.transpose(fields[3], (1, 0, 2))
    out_force[2] = jnp.transpose(fields[2], (1, 0, 2))


def spectral_fits(shape, counts):
    gx, gy, gz = counts
    nx, ny, nz = shape
    count = gx * gy * gz
    if ny % (2 * count) or ny != nx or nx != 2 * count or min(shape) < 2 * RADIUS + 2:
        return False
    return nz == 2 * LANES and gy == 2 and nx % (8 * gz) == 0


def spectral_shards(counts, density):
    gx, gy, gz = counts
    sx, sy, sz = density.shape
    dims = (sx * gz, sy * gx, sz * gy)
    count, group = gx * gy * gz, gy * gz
    pair = sy // group
    consts, scalars = tables(dims, count, gy, pair)
    for name in SPLIT:
        full = consts[name]
        high = full.astype(jnp.bfloat16)
        consts[name] = np.stack([high, (full - high.astype(np.float32)).astype(jnp.bfloat16)])
    scratch = {k: pltpu.VMEM(a.shape, a.dtype) for k, a in consts.items()}
    scratch["green"] = pltpu.VMEM(consts["green"].shape[1:], jnp.float32)
    scratch["density"] = pltpu.VMEM((sx, sy, sz), jnp.float32)
    scratch["scalars"] = pltpu.SMEM(scalars.shape, jnp.float32)
    given = {"density": density, "scalars": scalars, **consts}
    names = tuple(given)
    any_spec = pl.BlockSpec(memory_space=pl.ANY)
    vmem = pl.BlockSpec(memory_space=pltpu.VMEM)
    tile = (count, ROWS, LANES)
    slots = 7
    scratch = [scratch[k] for k in names]
    scratch += [
        pltpu.VMEM((sy, sx, sz), jnp.float32),
        pltpu.VMEM(tile, jnp.float32),
        pltpu.VMEM((gy, pair, gz, sx, LANES), jnp.float32),
        pltpu.VMEM(tile, jnp.float32),
        pltpu.VMEM((count, 1, LANES), jnp.float32),
        pltpu.VMEM((count, 1, LANES), jnp.float32),
        pltpu.VMEM((count, 2, ROWS, LANES), jnp.float32),
        pltpu.VMEM((count, 2, ROWS, LANES), jnp.float32),
        pltpu.VMEM(tile, jnp.float32),
        pltpu.VMEM(tile, jnp.float32),
        pltpu.VMEM((group, 4, pair, sx, LANES), jnp.float32),
        pltpu.SemaphoreType.DMA((len(names),)),
        pltpu.SemaphoreType.DMA((slots,)),
        pltpu.SemaphoreType.DMA((slots,)),
    ]
    fields = pl.pallas_call(
        functools.partial(spectral_kernel, dims + (gx, gy, gz), names),
        out_shape=pltpu.VMEM((4, sy, sx, sz), jnp.float32),
        in_specs=[any_spec] * len(names),
        out_specs=vmem,
        scratch_shapes=scratch,
        compiler_params=pltpu.CompilerParams(collective_id=0, has_side_effects=True),
    )(*[jnp.asarray(given[k]) for k in names])
    fields = pltpu.with_memory_space_constraint(fields, pltpu.VMEM)
    return pl.pallas_call(
        hand_out,
        out_shape=(
            jax.ShapeDtypeStruct((sx, sy, sz), jnp.float32),
            jax.ShapeDtypeStruct((3, sx, sy, sz), jnp.float32),
        ),
        in_specs=[vmem],
        out_specs=(vmem, vmem),
    )(fields)


def solution(mesh):
    counts = tuple(mesh.shape[a] for a in NAMES)

    def shards(density):
        sx, sy, sz = density.shape
        dims = (sx * counts[2], sy * counts[0], sz * counts[1])
        if spectral_fits(dims, counts):
            return spectral_shards(counts, density)
        return block_shards(density)

    return jax.shard_map(
        shards,
        mesh=mesh,
        in_specs=(P("gz", "gx", "gy"),),
        out_specs=(P("gz", "gx", "gy"), P(None, "gz", "gx", "gy")),
        check_vma=False,
    )
```

```python
import functools

import jax
import jax.numpy as jnp
import numpy as np
from jax import lax
from jax.experimental import pallas as pl
from jax.experimental.pallas import tpu as pltpu
from jax.sharding import PartitionSpec as P

RADIUS = 15
MARGIN = 16
SCREEN = 32


PRECISE = lax.Precision.HIGHEST
WEIGHTS = (1.0, 0.7, 0.5)
FRACTIONS = (0.5, 0.25, 0.125)
AMPLITUDE = 2.0
SMOOTHING = 1.0
TWO_PI = 6.283185307179586


def extended_2(cells, sides, width):
    for axis, dim in sides:
        count = lax.axis_size(axis)
        head = lax.slice_in_dim(cells, 0, width, axis=dim)
        tail = lax.slice_in_dim(cells, cells.shape[dim] - width, cells.shape[dim], axis=dim)
        cells = jnp.concatenate(
            [
                lax.ppermute(tail, axis, [(i, (i + 1) % count) for i in range(count)]),
                cells,
                lax.ppermute(head, axis, [((i + 1) % count, i) for i in range(count)]),
            ],
            axis=dim,
        )
    return cells


def profile(offset, spread):
    offsets = jnp.arange(-RADIUS, RADIUS + 1).astype(jnp.float32)
    norm_sum = jnp.sqrt(jnp.sum(jnp.exp(-offsets * offsets / (spread * spread))))
    inside = jnp.abs(offset) <= RADIUS
    return jnp.where(inside, jnp.exp(-offset * offset / (2.0 * spread * spread)), 0.0) / norm_sum


def band_pair(length, spread):
    rows_out = jnp.arange(length).astype(jnp.float32)[:, None]
    rows_in = jnp.arange(length + 2 * MARGIN).astype(jnp.float32)[None, :]
    offset = rows_out + MARGIN - rows_in
    smooth = profile(offset, spread)
    slope_part = -0.5 * (profile(offset + 1.0, spread) - profile(offset - 1.0, spread))
    return (smooth, slope_part)


def short_range(padded, size_x, size_y, size_z):
    mats_x = []
    mats_y = []
    mats_z = []
    for fraction, weight in zip(FRACTIONS, WEIGHTS):
        spread = RADIUS * fraction
        mats_x.append(jnp.stack(band_pair(size_x, spread)))
        mats_y.append(jnp.stack(band_pair(size_y, spread)))
        smooth_z, slope_z = band_pair(size_z, spread)
        mats_z.append(jnp.stack([weight * smooth_z, weight * slope_z]))
    stack_x = jnp.stack(mats_x)
    stack_y = jnp.stack(mats_y)
    stack_z = jnp.stack(mats_z)
    section_one = jnp.einsum("gsia,abc->gsibc", stack_x, padded, precision=PRECISE)
    section_two = jnp.einsum("gtjb,gibc->gtijc", stack_y, section_one[:, 0], precision=PRECISE)
    section_three = jnp.einsum(
        "gjb,gibc->gijc", stack_y[:, 0], section_one[:, 1], precision=PRECISE
    )
    smooth_pair = jnp.einsum("gijc,gtkc->tijk", section_two[:, 0], stack_z, precision=PRECISE)
    near_y = jnp.einsum("gijc,gkc->ijk", section_two[:, 1], stack_z[:, 0], precision=PRECISE)
    near_x = jnp.einsum("gijc,gkc->ijk", section_three, stack_z[:, 0], precision=PRECISE)
    return (smooth_pair[0], near_x, near_y, smooth_pair[1])


def unit_phase(product, modulus):
    angles = TWO_PI * (product % modulus).astype(jnp.float32) / modulus
    return (jnp.cos(angles), jnp.sin(angles))


def symbol(indices, length):
    angles = jnp.pi * indices.astype(jnp.float32) / length
    return (4.0 * jnp.sin(angles) ** 2, indices == length // 2, indices == 0)


def rotate(pattern, cos_t, sin_t, real_part, imag_part, direction):
    real_out = jnp.einsum(pattern, cos_t, real_part, precision=PRECISE) - direction * jnp.einsum(
        pattern, sin_t, imag_part, precision=PRECISE
    )
    imag_out = direction * jnp.einsum(pattern, sin_t, real_part, precision=PRECISE) + jnp.einsum(
        pattern, cos_t, imag_part, precision=PRECISE
    )
    return (real_out, imag_out)


def swap_rows(payload):
    return lax.all_to_all(payload, "gx", split_axis=2, concat_axis=2, tiled=True)


def swap_depth(payload):
    return lax.all_to_all(payload, "gz", split_axis=2, concat_axis=2, tiled=True)


def swap_columns(payload):
    return lax.all_to_all(payload, ("gx", "gy"), split_axis=2, concat_axis=2, tiled=True)


def long_range(density):
    size_x, size_y, size_z = density.shape
    count_gx = lax.axis_size("gx")
    count_gy = lax.axis_size("gy")
    count_gz = lax.axis_size("gz")
    local_x = size_x // 2
    local_y = size_y // 2
    local_z = size_z // 2
    depth_z = local_z // count_gx
    total_x = local_x * count_gz
    total_y = local_y * count_gx
    total_z = local_z * count_gy
    groups = count_gx * count_gy
    block_x = total_x // groups
    block_y = total_y // count_gz
    own_group = lax.axis_index("gx") * count_gy + lax.axis_index("gy")
    own_depth = lax.axis_index("gz")
    coarse = density.reshape(local_x, 2, local_y, 2, local_z, 2).mean(axis=(1, 3, 5))
    freq_y = jnp.arange(count_gz)[:, None] * block_y + jnp.arange(block_y)[None, :]
    pos_y = jnp.arange(count_gx)[:, None] * local_y + jnp.arange(local_y)[None, :]
    cos_y, sin_y = unit_phase(freq_y[:, :, None, None] * pos_y[None, None, :, :], total_y)
    rows_in = swap_rows(coarse.reshape(local_x, local_y, count_gx, depth_z))
    real_y = jnp.einsum("qrab,xbal->xqrl", cos_y, rows_in, precision=PRECISE)
    imag_y = -jnp.einsum("qrab,xbal->xqrl", sin_y, rows_in, precision=PRECISE)
    depth_in = swap_depth(jnp.stack([real_y, imag_y]))
    freq_x = jnp.arange(groups)[:, None] * block_x + jnp.arange(block_x)[None, :]
    pos_x = jnp.arange(count_gz)[:, None] * local_x + jnp.arange(local_x)[None, :]
    cos_x, sin_x = unit_phase(freq_x[:, :, None, None] * pos_x[None, None, :, :], total_x)
    real_x, imag_x = rotate("pscx,xcrl->sprl", cos_x, sin_x, depth_in[0], depth_in[1], -1.0)
    cols_in = swap_columns(jnp.stack([real_x, imag_x]))
    source = jnp.arange(groups)
    pos_z = (source % count_gy * local_z + source // count_gy * depth_z)[:, None] + jnp.arange(
        depth_z
    )[None, :]
    cos_z, sin_z = unit_phase(jnp.arange(total_z)[:, None, None] * pos_z[None, :, :], total_z)
    real_z, imag_z = rotate("kjl,sjrl->srk", cos_z, sin_z, cols_in[0], cols_in[1], -1.0)
    wave_x, edge_x, zero_x = symbol(own_group * block_x + jnp.arange(block_x), total_x)
    wave_y, edge_y, zero_y = symbol(own_depth * block_y + jnp.arange(block_y), total_y)
    wave_z, edge_z, zero_z = symbol(jnp.arange(total_z), total_z)
    kappa_sq = wave_x[:, None, None] + wave_y[None, :, None] + wave_z[None, None, :]
    dropped = edge_x[:, None, None] | edge_y[None, :, None] | edge_z[None, None, :]
    dropped = dropped | zero_x[:, None, None] & zero_y[None, :, None] & zero_z[None, None, :]
    green_fn = jnp.where(
        dropped,
        0.0,
        AMPLITUDE
        * jnp.exp(-SMOOTHING * SMOOTHING * kappa_sq)
        / (kappa_sq + 1.0 / (SCREEN * SCREEN)),
    )
    real_g = real_z * green_fn
    imag_g = imag_z * green_fn
    back_real, back_imag = rotate("kjl,srk->sjrl", cos_z, sin_z, real_g, imag_g, 1.0)
    cols_out = swap_columns(jnp.stack([back_real, back_imag]))
    real_b, imag_b = rotate("pscx,sprl->xcrl", cos_x, sin_x, cols_out[0], cols_out[1], 1.0)
    depth_out = swap_depth(jnp.stack([real_b, imag_b]))
    scale_y = jnp.ones(freq_y.shape, jnp.float32)
    result = jnp.einsum(
        "qrab,xqrl->xbal", cos_y * scale_y[:, :, None, None], depth_out[0], precision=PRECISE
    )
    result = result - jnp.einsum(
        "qrab,xqrl->xbal", sin_y * scale_y[:, :, None, None], depth_out[1], precision=PRECISE
    )
    result = result / (total_x * total_y * total_z)
    rows_out = swap_rows(result)
    return rows_out.reshape(local_x, local_y, local_z)


def transfer_pair(length):
    fine_cells = jnp.arange(-1, length + 1)
    parent = jnp.floor_divide(fine_cells, 2)
    parity = fine_cells - 2 * parent
    neighbour = parent - 1 + 2 * parity
    coarse_slots = jnp.arange(length // 2 + 2) - 1
    extended = 0.75 * (coarse_slots[None, :] == parent[:, None]).astype(jnp.float32)
    extended = extended + 0.25 * (coarse_slots[None, :] == neighbour[:, None]).astype(jnp.float32)
    value_map = extended[1 : length + 1]
    slope_map = -0.5 * (extended[2:] - extended[:-2])
    return (value_map, slope_map)


def prolong_brick(coarse_rims, size_x, size_y, size_z):
    value_x, slope_x = transfer_pair(size_x)
    value_y, slope_y = transfer_pair(size_y)
    value_z, slope_z = transfer_pair(size_z)
    along_z = jnp.einsum(
        "abe,tze->tabz", coarse_rims, jnp.stack([value_z, slope_z]), precision=PRECISE
    )
    level_y = jnp.einsum("aez,ye->ayz", along_z[0], value_y, precision=PRECISE)
    cross_y = jnp.einsum("aez,ye->ayz", along_z[0], slope_y, precision=PRECISE)
    cross_z = jnp.einsum("aez,ye->ayz", along_z[1], value_y, precision=PRECISE)
    far_pot = jnp.einsum("ayz,xa->xyz", level_y, value_x, precision=PRECISE)
    far_x = jnp.einsum("ayz,xa->xyz", level_y, slope_x, precision=PRECISE)
    far_y = jnp.einsum("ayz,xa->xyz", cross_y, value_x, precision=PRECISE)
    far_z = jnp.einsum("ayz,xa->xyz", cross_z, value_x, precision=PRECISE)
    return (far_pot, far_x, far_y, far_z)


def block_shards(density):
    size_x, size_y, size_z = density.shape
    padded = extended_2(density, (("gx", 1), ("gy", 2), ("gz", 0)), MARGIN)
    coarse_field = long_range(density)
    near_pot, near_x, near_y, near_z = short_range(padded, size_x, size_y, size_z)
    coarse_rims = extended_2(coarse_field, (("gx", 1), ("gy", 2), ("gz", 0)), 1)
    far_pot, far_x, far_y, far_z = prolong_brick(coarse_rims, size_x, size_y, size_z)
    potential = near_pot + far_pot
    forces = jnp.stack([near_x + far_x, near_y + far_y, near_z + far_z])
    return (potential, forces)


LANES = 128
ROWS = 8
NAMES = ("gx", "gy", "gz")


def cas(length):
    grid = np.outer(np.arange(length), np.arange(length)) % length
    angles = 2.0 * np.pi * grid / length
    return np.cos(angles) + np.sin(angles)


def averaging(length):
    out = np.zeros((length // 2, length))
    cells = np.arange(length // 2)
    out[cells, 2 * cells] = 0.5
    out[cells, 2 * cells + 1] = 0.5
    return out


def interpolation(length):
    half = length // 2
    out = np.zeros((length, half))
    cells = np.arange(half)
    out[2 * cells, cells] += 0.75
    out[2 * cells, (cells - 1) % half] += 0.25
    out[2 * cells + 1, cells] += 0.75
    out[2 * cells + 1, (cells + 1) % half] += 0.25
    return out


def slope_rows(values):
    return -0.5 * (np.roll(values, -1, 0) - np.roll(values, 1, 0))


def eigenvalues(length):
    offsets = np.arange(-RADIUS, RADIUS + 1)
    waves = np.cos(2.0 * np.pi * np.outer(np.arange(length), offsets) / length)
    out = []
    for fraction in FRACTIONS:
        spread = RADIUS * fraction
        norm = np.sqrt(np.sum(np.exp(-(offsets**2) / spread**2)))
        out.append(waves @ (np.exp(-(offsets**2) / (2.0 * spread**2)) / norm))
    return np.stack(out)


def green_table(sizes):
    waves = [4.0 * np.sin(np.pi * np.arange(m) / m) ** 2 for m in sizes]
    edges = [np.arange(m) == m // 2 for m in sizes]
    kappa = waves[0][:, None, None] + waves[1][None, :, None] + waves[2][None, None, :]
    dropped = edges[0][:, None, None] | edges[1][None, :, None] | edges[2][None, None, :]
    dropped[0, 0, 0] = True
    green = AMPLITUDE * np.exp(-SMOOTHING * SMOOTHING * kappa) / (kappa + 1.0 / SCREEN**2)
    return np.where(dropped, 0.0, green) / np.prod(sizes)


def tables(dims, count, halves, pair):
    nx, ny, nz = dims
    wide = nx // count
    hx, hy, hz = cas(nx), cas(ny), cas(nz)
    cx, cy, cz = cas(nx // 2), cas(ny // 2), cas(nz // 2)
    eye_h, eye_y, eye_k = np.eye(halves), np.eye(pair), np.eye(wide)
    side = halves * pair * nx
    out = {}
    out["hz"] = hz
    out["cz"] = (cz @ averaging(nz)).T
    out["lx"] = np.einsum("ab,yw,dkx->daykbwx", eye_h, eye_y, hx.reshape(count, wide, nx)).reshape(
        side, side
    )
    out["lxc"] = np.concatenate([cx @ averaging(nx) / pair] * pair, axis=1)
    out["ly"] = np.einsum("ab,kl,qsy->akqsbyl", eye_h, eye_k, hy.reshape(ny, count, pair)).reshape(
        side, side
    )
    out["lyc"] = cy
    fine = interpolation(ny) @ cy
    for name, level in (("value", hy), ("slope", slope_rows(hy))):
        out["by_" + name] = np.einsum(
            "ab,kl,syq->saykblq", eye_h, eye_k, level.reshape(count, pair, ny)
        ).reshape(side, side)
    level = np.zeros((count, ROWS, ny // 2))
    level[:, :pair] = fine.reshape(count, pair, -1)
    level[:, pair : 2 * pair] = slope_rows(fine).reshape(count, pair, -1)
    out["byc"] = level.reshape(count * ROWS, -1)
    out["bx"] = np.einsum("ab,yw,xdk->ayxdbwk", eye_h, eye_y, hx.reshape(nx, count, wide)).reshape(
        side, side
    )
    back = np.zeros((2 * pair, nx, count, ROWS))
    for row in range(2 * pair):
        back[row, :, :, row] = interpolation(nx) @ cx
    out["bxc"] = back.reshape(2 * pair * nx, count * ROWS)
    out["bzc"] = (interpolation(nz) @ cz).T
    ev_y, ev_z = eigenvalues(ny), eigenvalues(nz)
    weights = np.array(WEIGHTS) / (nx * ny * nz)
    plane = np.einsum("g,gy,gz->gyz", weights, ev_y, ev_z)
    out["plane"] = plane.reshape(len(WEIGHTS), ny, halves, LANES).transpose(0, 2, 1, 3)
    out["green"] = green_table((nx // 2, ny // 2, nz // 2))
    scalars = eigenvalues(nx).T.reshape(-1).astype(np.float32)
    return {k: np.asarray(v, np.float32) for k, v in out.items()}, scalars


def halves_of(values):
    high = values.astype(jnp.bfloat16)
    return high, (values - high.astype(jnp.float32)).astype(jnp.bfloat16)


SPLIT = ("hz", "cz", "lx", "lxc", "ly", "lyc", "by_value", "by_slope", "byc", "bx", "bxc", "bzc")


def dot(a, b):
    a_high, a_low = a if isinstance(a, tuple) else halves_of(a)
    b_high, b_low = b if isinstance(b, tuple) else halves_of(b)
    out = jnp.dot(a_high, b_low, preferred_element_type=jnp.float32)
    out = out + jnp.dot(a_low, b_high, preferred_element_type=jnp.float32)
    return out + jnp.dot(a_high, b_high, preferred_element_type=jnp.float32)


def spectral_kernel(shape, names, *refs):
    nx, ny, nz, gx, gy, gz = shape
    group, count = gy * gz, gx * gy * gz
    wide = nx // count
    n = len(names)
    hbm = dict(zip(names, refs[:n]))
    recv_e = refs[n]
    tab = dict(zip(names, refs[n + 1 : 2 * n + 1]))
    (
        turned,
        send_b,
        recv_a,
        recv_b,
        send_c,
        recv_c,
        send_d,
        recv_d,
        send_s,
        recv_s,
        send_e,
        tab_sem,
        sems,
        semr,
    ) = refs[2 * n + 1 :]
    ix, iy, iz = lax.axis_index("gx"), lax.axis_index("gy"), lax.axis_index("gz")
    mine = iz * gy + iy
    me = ix * group + mine
    pair = recv_a.shape[1]
    edge = recv_a.shape[3]

    def where(p):
        return {"gx": p // group, "gy": p % gy, "gz": (p % group) // gy}

    barrier = pltpu.get_barrier_semaphore()

    def greet(j, carry):
        pl.semaphore_signal(
            barrier, inc=1, device_id=where((me + j) % count), device_id_type=pl.DeviceIdType.MESH
        )
        return carry

    lax.fori_loop(1, count, greet, 0, unroll=True)

    loads = {}
    for i, name in enumerate(names):
        source = hbm[name].at[me] if name == "green" else hbm[name]
        loads[name] = pltpu.make_async_copy(source, tab[name], tab_sem.at[i])
        loads[name].start()

    def table(name):
        if name in loads:
            loads.pop(name).wait()
        values = tab[name]
        return (values[0], values[1]) if name in SPLIT else values

    scal = tab["scalars"]
    turned[...] = jnp.transpose(table("density")[...], (1, 0, 2))
    pl.semaphore_wait(barrier, count - 1)

    def remote(src, dst, slot, p):
        return pltpu.make_async_remote_copy(
            src_ref=src,
            dst_ref=dst,
            send_sem=sems.at[slot],
            recv_sem=semr.at[slot],
            device_id=where(p),
            device_id_type=pl.DeviceIdType.MESH,
        )

    def group_exchange(slot, source, target, some_source, some_target):
        for j in range(1, group):
            other = (mine + j) % group
            remote(source(other), target(mine), slot, ix * group + other).start()
        total = remote(some_source, some_target, slot, ix * group + (mine + 1) % group)
        return total.wait_recv, total.wait_send

    def full_exchange(slot, source, target):
        for k in sorted(range(gx), key=lambda k: -min(k, gx - k)):
            for m in range(group):
                if k or m:
                    other = (ix + k) % gx * group + (mine + m) % group
                    remote(source.at[other], target.at[me], slot, other).start()
        rest = pl.ds(0, count - 1)
        total = remote(source.at[rest], target.at[rest], slot, (me + 1) % count)
        return total.wait_recv, total.wait_send

    pending = []
    arrive, sent = group_exchange(
        0,
        lambda h: turned.at[pl.ds(h * pair, pair)],
        lambda h: recv_a.at[h % gy, :, h // gy],
        turned.at[pl.ds(0, (group - 1) * pair)],
        turned.at[pl.ds(0, (group - 1) * pair)],
    )
    pending.append(sent)
    recv_a[iy, :, iz] = turned[pl.ds(mine * pair, pair)]
    hz, cz, lx, lxc = table("hz"), table("cz"), table("lx"), table("lxc")
    arrive()
    cells = halves_of(
        jnp.concatenate([recv_a[h].reshape(pair * nx, LANES) for h in range(gy)], axis=1)
    )
    along = dot(cells, hz)
    along = jnp.concatenate([along[:, h * LANES : (h + 1) * LANES] for h in range(gy)], axis=0)
    send_b[...] = dot(lx, along).reshape(send_b.shape)
    arrive_b, sent = full_exchange(1, send_b, recv_b)
    pending.append(sent)
    send_c[:, 0, :] = dot(lxc, dot(cells, cz))
    arrive_c, sent = full_exchange(2, send_c, recv_c)
    pending.append(sent)
    recv_b[me] = send_b[me]
    recv_c[me] = send_c[me]
    table("scalars")
    plane = table("plane")
    responses = []
    for h in range(gy):
        for k in range(wide):
            responses.append(
                sum(
                    scal[(me * wide + k) * len(WEIGHTS) + g] * plane[g, h]
                    for g in range(len(WEIGHTS))
                )
            )
    response = jnp.concatenate(responses, axis=0)
    ly, lyc, green = table("ly"), table("lyc"), table("green")
    by_value, by_slope, byc = table("by_value"), table("by_slope"), table("byc")
    arrive_b()
    spectrum = dot(ly, recv_b[...].reshape(count * ROWS, LANES)) * response
    spectrum = halves_of(spectrum)
    send_d[:, 0] = dot(by_value, spectrum).reshape(send_b.shape)
    arrive_c()
    coarse = dot(lyc, recv_c[:, 0, :]) * green[...]
    send_d[:, 1] = dot(byc, coarse).reshape(send_b.shape)
    arrive_d, sent = full_exchange(3, send_d, recv_d)
    pending.append(sent)
    send_s[...] = dot(by_slope, spectrum).reshape(send_b.shape)
    arrive_s, sent = full_exchange(4, send_s, recv_s)
    pending.append(sent)
    recv_d[me] = send_d[me]
    recv_s[me] = send_s[me]
    bx, bxc, bzc = table("bx"), table("bxc"), table("bzc")
    size = pair * nx

    def near_part(received):
        level = dot(bx, received.reshape(count * ROWS, LANES))
        level = jnp.concatenate([level[h * size : (h + 1) * size] for h in range(gy)], axis=1)
        return dot(level, hz)

    def place(f, y, field):
        for a in range(gz):
            for b in range(gy):
                send_e[a * gy + b, f, y] = field[
                    a * edge : (a + 1) * edge, b * LANES : (b + 1) * LANES
                ]

    arrive_d()
    far = dot(dot(bxc, recv_d[:, 1].reshape(count * ROWS, LANES)), bzc)
    values = near_part(recv_d[:, 0]) + far[:size]
    for y in range(pair):
        pot = values[y * nx : (y + 1) * nx]
        place(0, y, pot)
        place(1, y, -0.5 * (pltpu.roll(pot, nx - 1, 0) - pltpu.roll(pot, 1, 0)))
        place(2, y, -0.5 * (pltpu.roll(pot, nz - 1, 1) - pltpu.roll(pot, 1, 1)))
    arrive_v, sent = group_exchange(
        5,
        lambda h: send_e.at[h, pl.ds(0, 3)],
        lambda h: recv_e.at[pl.ds(0, 3), pl.ds(h * pair, pair)],
        send_e.at[pl.ds(0, group - 1), pl.ds(0, 3)],
        send_e.at[pl.ds(0, group - 1), pl.ds(0, 3)],
    )
    pending.append(sent)
    arrive_s()
    slopes = near_part(recv_s[...]) + far[size:]
    for y in range(pair):
        place(3, y, slopes[y * nx : (y + 1) * nx])
    arrive_y, sent = group_exchange(
        6,
        lambda h: send_e.at[h, 3],
        lambda h: recv_e.at[3, pl.ds(h * pair, pair)],
        send_e.at[pl.ds(0, group - 1), 3],
        send_e.at[pl.ds(0, group - 1), 3],
    )
    pending.append(sent)
    recv_e[:, pl.ds(mine * pair, pair)] = send_e[mine]
    arrive_v()
    arrive_y()
    for sent in pending:
        sent()


def hand_out(fields, out_pot, out_force):
    out_pot[...] = jnp.transpose(fields[0], (1, 0, 2))
    out_force[0] = jnp.transpose(fields[1], (1, 0, 2))
    out_force[1] = jnp.transpose(fields[3], (1, 0, 2))
    out_force[2] = jnp.transpose(fields[2], (1, 0, 2))


def spectral_fits(shape, counts):
    gx, gy, gz = counts
    nx, ny, nz = shape
    count = gx * gy * gz
    if ny % (2 * count) or ny != nx or nx != 2 * count or min(shape) < 2 * RADIUS + 2:
        return False
    return nz == 2 * LANES and gy == 2 and nx % (8 * gz) == 0


def spectral_shards(counts, density):
    gx, gy, gz = counts
    sx, sy, sz = density.shape
    dims = (sx * gz, sy * gx, sz * gy)
    count, group = gx * gy * gz, gy * gz
    pair = sy // group
    consts, scalars = tables(dims, count, gy, pair)
    for name in SPLIT:
        full = consts[name]
        high = full.astype(jnp.bfloat16)
        consts[name] = np.stack([high, (full - high.astype(np.float32)).astype(jnp.bfloat16)])
    scratch = {k: pltpu.VMEM(a.shape, a.dtype) for k, a in consts.items()}
    scratch["green"] = pltpu.VMEM(consts["green"].shape[1:], jnp.float32)
    scratch["density"] = pltpu.VMEM((sx, sy, sz), jnp.float32)
    scratch["scalars"] = pltpu.SMEM(scalars.shape, jnp.float32)
    given = {"density": density, "scalars": scalars, **consts}
    names = tuple(given)
    any_spec = pl.BlockSpec(memory_space=pl.ANY)
    vmem = pl.BlockSpec(memory_space=pltpu.VMEM)
    tile = (count, ROWS, LANES)
    slots = 7
    scratch = [scratch[k] for k in names]
    scratch += [
        pltpu.VMEM((sy, sx, sz), jnp.float32),
        pltpu.VMEM(tile, jnp.float32),
        pltpu.VMEM((gy, pair, gz, sx, LANES), jnp.float32),
        pltpu.VMEM(tile, jnp.float32),
        pltpu.VMEM((count, 1, LANES), jnp.float32),
        pltpu.VMEM((count, 1, LANES), jnp.float32),
        pltpu.VMEM((count, 2, ROWS, LANES), jnp.float32),
        pltpu.VMEM((count, 2, ROWS, LANES), jnp.float32),
        pltpu.VMEM(tile, jnp.float32),
        pltpu.VMEM(tile, jnp.float32),
        pltpu.VMEM((group, 4, pair, sx, LANES), jnp.float32),
        pltpu.SemaphoreType.DMA((len(names),)),
        pltpu.SemaphoreType.DMA((slots,)),
        pltpu.SemaphoreType.DMA((slots,)),
    ]
    fields = pl.pallas_call(
        functools.partial(spectral_kernel, dims + (gx, gy, gz), names),
        out_shape=pltpu.VMEM((4, sy, sx, sz), jnp.float32),
        in_specs=[any_spec] * len(names),
        out_specs=vmem,
        scratch_shapes=scratch,
        compiler_params=pltpu.CompilerParams(collective_id=0, has_side_effects=True),
    )(*[jnp.asarray(given[k]) for k in names])
    fields = pltpu.with_memory_space_constraint(fields, pltpu.VMEM)
    return pl.pallas_call(
        hand_out,
        out_shape=(
            jax.ShapeDtypeStruct((sx, sy, sz), jnp.float32),
            jax.ShapeDtypeStruct((3, sx, sy, sz), jnp.float32),
        ),
        in_specs=[vmem],
        out_specs=(vmem, vmem),
    )(fields)


def solution(mesh):
    counts = tuple(mesh.shape[a] for a in NAMES)

    def shards(density):
        sx, sy, sz = density.shape
        dims = (sx * counts[2], sy * counts[0], sz * counts[1])
        if spectral_fits(dims, counts):
            return spectral_shards(counts, density)
        return block_shards(density)

    return jax.shard_map(
        shards,
        mesh=mesh,
        in_specs=(P("gz", "gx", "gy"),),
        out_specs=(P("gz", "gx", "gy"), P(None, "gz", "gx", "gy")),
        check_vma=False,
    )
```
